256 devices in a mesh: slab: 64 (over y, x, z_hi), pt: 4 (over z_lo, core).
Axes of the slice: x: 4, y: 4, z: 8 (z_hi: 4, z_lo: 2; z = z_hi * 2 + z_lo), core: 2. Of those that a mesh axis runs over, the one named last changes fastest.
Arguments:
- orbitals: bfloat16 [131072, 256], P('slab'), may hold values from -6 to 6
- potential: float32 [131072], P('slab'), may hold values from -1 to 1
- fit_matrix: bfloat16 [131072, 8192], P('slab', 'pt'), may hold values from -0.00390625 to 0.00390625
- owner_rows: int32 [4, 64, 64], P(None, 'slab'), may hold values from 0 to 2047, as said below
- owner_count: int32 [4, 64], replicated, may hold values from 0 to 64, as said below
Outputs:
- filtered: bfloat16 [131072, 256], P('slab')
The draws below stay inside these ranges and needn't reach their ends.
Inputs may be any that keep to these rules, and one draw needn't show every extreme that they name: `owner_count`: for each block p the counts over slabs sum to 2048, and in every block some slab lists exactly 64 points. `owner_rows`: the listed entries (c < owner_count[p, s]) of slab s are distinct over all blocks p and slots c; the other entries are 0.
All inputs are finite; a program needn't handle non-finite values.
Results may differ from the reference program's by a relative error of at most 0.0054.
Values may be sent and summed in bfloat16 or wider, within the bound.
No kernel may reach another device: no remote copies, remote signals or barrier semaphores. Data moves between devices by JAX's collectives and lax.ppermute only.
A program may use at most 64 MiB of HBM per device.

```python
import jax
import jax.numpy as jnp
from jax import lax

NB = 256
NMU = 8192
DEG = 2
CZ = 8
NY = 8
NX = 32
G_DEV = 2048
NG = 131072
NMU_DEV = 2048
CAP = 64
N_SLAB = 64
N_PT = 4


def owner_layout(key):
    base_key = jax.random.fold_in(key, 7)
    key_big, key_weight, key_score, key_perm = jax.random.split(base_key, 4)
    slab_ids = jnp.arange(N_SLAB, dtype=jnp.int32)
    busiest = jax.random.randint(key_big, (N_PT,), 0, N_SLAB)
    is_big = slab_ids[None, :] == busiest[:, None]
    weights = jnp.where(is_big, 0, jax.random.randint(key_weight, (N_PT, N_SLAB), 2, 4))
    remaining = NMU_DEV - CAP
    shares = weights * remaining // jnp.sum(weights, axis=1, keepdims=True)
    leftover = remaining - jnp.sum(shares, axis=1, keepdims=True)
    scores = jax.random.randint(key_score, (N_PT, N_SLAB), 0, 1 << 20) * N_SLAB + slab_ids[None, :]
    scores = jnp.where(is_big, (1 << 20) * N_SLAB, scores)
    ranking = jnp.argsort(jnp.argsort(scores, axis=1), axis=1)
    counts = jnp.where(is_big, CAP, shares + (ranking < leftover).astype(jnp.int32)).astype(jnp.int32)

    def one_perm(perm_key):
        return jax.random.permutation(perm_key, G_DEV)
    permuted = jax.vmap(one_perm)(jax.random.split(key_perm, N_SLAB))
    starts = jnp.cumsum(counts, axis=0) - counts
    slot_ids = jnp.arange(CAP, dtype=jnp.int32)
    take_at = jnp.minimum(starts[:, :, None] + slot_ids[None, None, :], G_DEV - 1)
    picked = permuted[slab_ids[None, :, None], take_at]
    chosen = jnp.where(slot_ids[None, None, :] < counts[:, :, None], picked, 0)
    return (counts, chosen.astype(jnp.int32))


def draw_owner_rows(key, part):
    return owner_layout(key)[1]


def draw_owner_count(key, part):
    return owner_layout(key)[0]


def block_levels(rng, extent, cuts, smallest, largest):
    loudness = 1.0
    for position, blocks in cuts:
        draws = jax.random.uniform(jax.random.fold_in(jax.random.fold_in(rng, 6), position), (blocks,), jnp.float32, smallest / len(cuts), largest / len(cuts))
        loudness = loudness * jnp.repeat(jnp.exp(draws), extent[position] // blocks).reshape((-1,) + (1,) * (len(extent) - 1 - position))
    return loudness


def noise(own_key, extent, scale, limit, cuts=(), kind=jnp.bfloat16):
    values = jax.random.normal(own_key, extent, jnp.float32) * scale
    if len(cuts) > 0:
        values = block_levels(own_key, extent, cuts, -0.22, 0.18) * values
    return jnp.clip(values, min=-limit, max=limit).astype(kind)


def setup_inputs(seed: int = 0) -> dict:
    keys = jax.random.split(jax.random.key(seed), 6)
    orbitals = noise(keys[0], (NG, NB), 1.0, 6.0, ((0, 64),))
    potential = jnp.clip(jax.random.uniform(keys[1], (NG,), jnp.float32, -1.0, 1.0) * block_levels(keys[1], (NG,), ((0, 64),), -0.4, 0.0), -1.0, 1.0)
    fit_matrix = noise(keys[2], (NG, NMU), (NMU * NB) ** -0.5, 0.00390625, ((0, 64), (1, 4)))
    owner_rows = draw_owner_rows(jax.random.fold_in(keys[5], 71), 0)
    owner_count = draw_owner_count(jax.random.fold_in(keys[5], 71), 0)
    return dict(orbitals=orbitals, potential=potential, fit_matrix=fit_matrix, owner_rows=owner_rows, owner_count=owner_count)


stencil_coef = (-205.0 / 72.0, 8.0 / 5.0, -1.0 / 5.0, 8.0 / 315.0, -1.0 / 560.0)


def kinetic(vectors):
    blocked = vectors.astype(jnp.float32).reshape(CZ * N_SLAB, NY, NX, NB)
    summed = 3.0 * stencil_coef[0] * blocked
    for offset in range(1, 5):
        for axis_num in range(3):
            summed = summed + stencil_coef[offset] * (jnp.roll(blocked, offset, axis_num) + jnp.roll(blocked, -offset, axis_num))
    return (-0.5 * summed).reshape(CZ * N_SLAB * NY * NX, NB)


def point_index(owner_rows, owner_count):
    inclusive = jnp.cumsum(owner_count, axis=1).astype(jnp.int32)
    point_ranks = jnp.arange(NMU // N_PT, dtype=jnp.int32)
    before = (inclusive[:, None, :] <= point_ranks[None, :, None]).astype(jnp.int32)
    slab_of = jnp.sum(before, axis=2).astype(jnp.int32)
    base_count = jnp.sum(before * owner_count[:, None, :], axis=2).astype(jnp.int32)
    flat_rows = owner_rows.reshape(N_PT, N_SLAB * CAP)
    local_rows = jnp.take_along_axis(flat_rows, (slab_of * CAP + point_ranks[None, :] - base_count).astype(jnp.int32), axis=1)
    return (slab_of * (CZ * NY * NX) + local_rows).reshape(NMU).astype(jnp.int32)


def reference(orbitals, potential, fit_matrix, owner_rows, owner_count):
    slab_rows = CZ * NY * NX
    points = point_index(owner_rows, owner_count)
    psi_points = jnp.take(orbitals, points, axis=0).astype(jnp.float32)
    orbital_blocks = orbitals.reshape(N_SLAB, slab_rows, NB)
    fit_blocks = fit_matrix.reshape(N_SLAB, slab_rows, NMU)

    def kernel_block(tile_pair):
        fit_block, orbital_block = tile_pair
        density = jnp.dot(orbital_block.astype(jnp.float32), psi_points.T, preferred_element_type=jnp.float32)
        return (fit_block.astype(jnp.float32) * density).astype(jnp.bfloat16)

    kernel = lax.map(kernel_block, (fit_blocks, orbital_blocks))

    def apply_op(vectors):
        field_points = jnp.take(vectors, points, axis=0).astype(jnp.float32)

        def exch_block(kernel_tile):
            return jnp.dot(kernel_tile.astype(jnp.float32), field_points, preferred_element_type=jnp.float32)

        exch_term = lax.map(exch_block, kernel).reshape(N_SLAB * slab_rows, NB)
        return kinetic(vectors) + potential[:, None] * vectors.astype(jnp.float32) - exch_term

    previous = orbitals
    current = orbitals
    for turn_number in range(DEG):
        applied = apply_op(current)
        scaled = applied - 3.5 * current.astype(jnp.float32)
        if turn_number == 0:
            upcoming = (scaled / 4.0).astype(jnp.bfloat16)
        else:
            upcoming = (0.5 * scaled - previous.astype(jnp.float32)).astype(jnp.bfloat16)
        previous, current = current, upcoming
    return current
```

```python
import functools

import jax
import jax.numpy as jnp
from jax import lax
from jax.experimental import pallas as pl
from jax.experimental.pallas import tpu as pltpu
from jax.sharding import PartitionSpec as P

NB = 256
HALF = 128
CZ = 8
NY = 8
NX = 32
PLANE = NY * NX
ROWS = CZ * PLANE
PTS = 2048
CAP = 64
WIN = 272
TILE = 256
STEPS = ROWS // TILE
BF = jnp.bfloat16
F32 = jnp.float32

stencil_coef = (-205.0 / 72.0, 8.0 / 5.0, -1.0 / 5.0, 8.0 / 315.0, -1.0 / 560.0)


def slab_id(y, x, z):
    return ((y % 4) * 4 + (x % 4)) * 4 + (z % 4)


def z_shift(d):
    return [(slab_id(y, x, z), slab_id(y, x, z - d)) for y in range(4) for x in range(4) for z in range(4)]


XY_GROUPS = [[slab_id(y, x, z) for y in range(4) for x in range(4)] for z in range(4)]
CORE_SWAP = [(i, i ^ 1) for i in range(4)]
CHIP_SWAP = [(i, i ^ 2) for i in range(4)]
EDGE_SWAP = [(s * 4 + 2 + c, ((s + 1) % 64) * 4 + c) for s in range(64) for c in range(2)] + [
    (s * 4 + c, ((s - 1) % 64) * 4 + 2 + c) for s in range(64) for c in range(2)
]


def plane_table():
    cell_ids = jnp.arange(PLANE, dtype=jnp.int32)
    row_y = cell_ids // NX
    col_x = cell_ids % NX
    diff_y = (row_y[:, None] - row_y[None, :]) % NY
    diff_x = (col_x[:, None] - col_x[None, :]) % NX
    same_y = row_y[:, None] == row_y[None, :]
    same_x = col_x[:, None] == col_x[None, :]
    table = jnp.zeros((PLANE, PLANE), F32)
    for offset in range(1, 5):
        along_x = (same_y & (diff_x == offset % NX)).astype(F32) + (same_y & (diff_x == -offset % NX)).astype(F32)
        along_y = (same_x & (diff_y == offset % NY)).astype(F32) + (same_x & (diff_y == -offset % NY)).astype(F32)
        table = table + stencil_coef[offset] * (along_x + along_y)
    return table


def local_terms(lower, own, upper, potential):
    planes = jnp.concatenate([lower, own, upper], axis=0).reshape(12, PLANE, HALF).astype(F32)
    center = own.reshape(4, PLANE, HALF).astype(F32)
    in_plane = jnp.einsum(
        "pq,zqb->zpb", plane_table(), center, precision=lax.Precision.HIGHEST, preferred_element_type=F32
    )
    summed = 3.0 * stencil_coef[0] * center + in_plane
    for offset in range(1, 5):
        summed = summed + stencil_coef[offset] * (planes[4 + offset : 8 + offset] + planes[4 - offset : 8 - offset])
    return (-0.5 * summed).reshape(1024, HALF) + potential[:, None] * own.astype(F32)


def pick_kernel(rows_ref, field_ref, out_ref):
    cols = lax.broadcasted_iota(jnp.int32, (CAP, ROWS), 1)
    hot = jnp.where(rows_ref[...] == cols, 1.0, 0.0).astype(BF)
    out_ref[...] = jnp.dot(hot, field_ref[...], preferred_element_type=F32).astype(BF)


def pick_rows(rows, field):
    return pl.pallas_call(
        pick_kernel, out_shape=jax.ShapeDtypeStruct((CAP, NB), BF), name="pick_rows"
    )(rows, field)


def compact(base_ref, where_ref, got_ref, sum_ref, psi_ref):
    sum_ref[...] = jnp.zeros_like(sum_ref)
    line = lax.broadcasted_iota(jnp.int32, (WIN, TILE), 0)
    for g in range(16):
        hot = jnp.where(where_ref[g : g + 1, :] == line, 1.0, 0.0).astype(BF)
        placed = jnp.dot(hot, got_ref[g], preferred_element_type=F32)
        at = pl.multiple_of(base_ref[g], 8)
        sum_ref[pl.ds(at, WIN), :] += placed
    psi_ref[...] = sum_ref[pl.ds(0, PTS), :].astype(BF)


def first_kernel(base_ref, where_ref, got_ref, orb_ref, fit_ref, local_ref, rows_ref,
                 kern_ref, keep_ref, send_ref, pick_ref, sum_ref, psi_ref, acc_ref):
    step = pl.program_id(0)
    core = base_ref[16]
    chip = base_ref[17]

    @pl.when(step == 0)
    def _():
        compact(base_ref, where_ref, got_ref, sum_ref, psi_ref)
        acc_ref[...] = jnp.zeros_like(acc_ref)

    density = lax.dot_general(
        orb_ref[...], psi_ref[...], (((1,), (1,)), ((), ())), preferred_element_type=F32
    )
    kern = (fit_ref[...].astype(F32) * density).astype(BF)
    kern_ref[...] = kern
    part = -jnp.dot(kern, psi_ref[...], preferred_element_type=F32)
    left, right = part[:, :HALF], part[:, HALF:]
    keep_ref[...] = jnp.where(core == 0, left, right)
    send_ref[...] = jnp.where(core == 0, right, left).astype(BF)
    local = local_ref[pl.ds(pl.multiple_of((step % 4) * TILE, TILE), TILE), :]
    local = jnp.where(step // 4 == chip, local, 0.0)
    whole = jnp.concatenate(
        [left + jnp.where(core == 0, local, 0.0), right + jnp.where(core == 0, 0.0, local)], axis=1
    ).astype(BF)
    lanes = lax.broadcasted_iota(jnp.int32, (4 * CAP, TILE), 1) + step * TILE
    hot = jnp.where(rows_ref[...] == lanes, 1.0, 0.0).astype(BF)
    acc_ref[...] += jnp.dot(hot, whole, preferred_element_type=F32)

    @pl.when(step == STEPS - 1)
    def _():
        pick_ref[...] = acc_ref[...].astype(BF)


def whole_block(shape):
    return pl.BlockSpec(shape, lambda i, *_: (0,) * len(shape))


def row_block(cols):
    return pl.BlockSpec((TILE, cols), lambda i, *_: (i, 0))


def first_apply(base, where, got, orbitals, fit_matrix, local, rows):
    return pl.pallas_call(
        first_kernel,
        name="first_apply",
        grid_spec=pltpu.PrefetchScalarGridSpec(
            num_scalar_prefetch=1,
            grid=(STEPS,),
            in_specs=[
                whole_block((16, TILE)),
                whole_block((16, TILE, NB)),
                row_block(NB),
                row_block(PTS),
                whole_block((1024, HALF)),
                whole_block((4 * CAP, 1)),
            ],
            out_specs=[row_block(PTS), row_block(HALF), row_block(HALF), whole_block((4 * CAP, NB))],
            scratch_shapes=[
                pltpu.VMEM((PTS + WIN, NB), F32),
                pltpu.VMEM((PTS, NB), BF),
                pltpu.VMEM((4 * CAP, NB), F32),
            ],
        ),
        out_shape=[
            jax.ShapeDtypeStruct((ROWS, PTS), BF),
            jax.ShapeDtypeStruct((ROWS, HALF), F32),
            jax.ShapeDtypeStruct((ROWS, HALF), BF),
            jax.ShapeDtypeStruct((4 * CAP, NB), BF),
        ],
    )(base, where, got, orbitals, fit_matrix, local, rows)


def second_kernel(base_ref, where_ref, got_ref, kern_ref, keep_ref, send_ref, sum_ref, psi_ref):
    core = base_ref[16]

    @pl.when(pl.program_id(0) == 0)
    def _():
        compact(base_ref, where_ref, got_ref, sum_ref, psi_ref)

    part = -jnp.dot(kern_ref[...], psi_ref[...], preferred_element_type=F32)
    left, right = part[:, :HALF], part[:, HALF:]
    keep_ref[...] = jnp.where(core == 0, left, right)
    send_ref[...] = jnp.where(core == 0, right, left).astype(BF)


def second_apply(base, where, got, kern):
    return pl.pallas_call(
        second_kernel,
        name="second_apply",
        grid_spec=pltpu.PrefetchScalarGridSpec(
            num_scalar_prefetch=1,
            grid=(STEPS,),
            in_specs=[whole_block((16, TILE)), whole_block((16, TILE, NB)), row_block(PTS)],
            out_specs=[row_block(HALF), row_block(HALF)],
            scratch_shapes=[pltpu.VMEM((PTS + WIN, NB), F32), pltpu.VMEM((PTS, NB), BF)],
        ),
        out_shape=[jax.ShapeDtypeStruct((ROWS, HALF), F32), jax.ShapeDtypeStruct((ROWS, HALF), BF)],
    )(base, where, got, kern)


def gather_points(own):
    along_z = [own] + [lax.ppermute(own, "slab", z_shift(d)) for d in (1, 2, 3)]
    column = jnp.concatenate(along_z, axis=0)
    spread = jnp.broadcast_to(column[None], (16, TILE, NB))
    return lax.all_to_all(spread, "slab", 0, 0, axis_index_groups=XY_GROUPS)


def body(orbitals, potential, fit_matrix, owner_rows, owner_count):
    point_block = lax.axis_index("pt")
    slab = lax.axis_index("slab")
    core = point_block % 2
    chip = point_block // 2
    my_z = slab % 4
    row0 = chip * 1024

    mine_rows = lax.dynamic_index_in_dim(owner_rows[:, 0, :], point_block, 0, keepdims=False)
    own0 = pick_rows(mine_rows.reshape(CAP, 1), orbitals)
    got0 = gather_points(own0)

    counts = lax.dynamic_index_in_dim(owner_count, point_block, 0, keepdims=False)
    group = jnp.arange(16, dtype=jnp.int32)
    slabs = group[:, None] * 4 + (my_z + jnp.arange(4, dtype=jnp.int32)[None, :]) % 4
    every = jnp.arange(64, dtype=jnp.int32)
    start = jnp.sum(jnp.where(every < slabs[:, :, None], counts, 0), axis=2)
    size = jnp.sum(jnp.where(every == slabs[:, :, None], counts, 0), axis=2)
    base = jnp.sum(jnp.where(every[None, :] < group[:, None] * 4, counts, 0), axis=1) // 8 * 8
    slot = jnp.arange(CAP, dtype=jnp.int32)
    where = jnp.where(slot < size[:, :, None], start[:, :, None] - base[:, None, None] + slot, -1).reshape(16, TILE)
    base = jnp.concatenate([base, core[None], chip[None]]).astype(jnp.int32)
    all_rows = owner_rows.reshape(4 * CAP, 1)

    def quadrant(field):
        return lax.dynamic_slice(field, (row0, core * HALF), (1024, HALF))

    potential_piece = lax.dynamic_slice(potential, (row0,), (1024,))
    field0 = quadrant(orbitals)
    inner0 = lax.dynamic_slice(orbitals, ((1 - chip) * 1024, core * HALF), (1024, HALF))

    def stencil(field, inner):
        outer = lax.ppermute(field, ("slab", "pt"), EDGE_SWAP)
        lower = jnp.where(chip == 0, outer, inner)
        upper = jnp.where(chip == 0, inner, outer)
        return local_terms(lower, field, upper, potential_piece)

    local0 = stencil(field0, inner0)

    kern, keep0, send0, picked = first_apply(base, where, got0, orbitals, fit_matrix, local0, all_rows)

    pieces = lax.all_to_all(picked.reshape(4, CAP, NB), "pt", 0, 0)
    applied = jnp.sum(pieces.astype(F32), axis=0)
    own1 = ((applied - 3.5 * own0.astype(F32)) / 4.0).astype(BF)
    got1 = gather_points(own1)

    def reduce_piece(keep, send):
        columns = keep + lax.ppermute(send, "pt", CORE_SWAP).astype(F32)
        away = lax.dynamic_slice(columns, ((1 - chip) * 1024, 0), (1024, HALF)).astype(BF)
        return lax.dynamic_slice(columns, (row0, 0), (1024, HALF)) + lax.ppermute(away, "pt", CHIP_SWAP).astype(F32)

    applied0 = local0 + reduce_piece(keep0, send0)
    field1 = ((applied0 - 3.5 * field0.astype(F32)) / 4.0).astype(BF)
    local1 = stencil(field1, lax.ppermute(field1, "pt", CHIP_SWAP))

    keep1, send1 = second_apply(base, where, got1, kern)
    applied1 = local1 + reduce_piece(keep1, send1)
    field2 = (0.5 * (applied1 - 3.5 * field1.astype(F32)) - field0.astype(F32)).astype(BF)

    other = lax.ppermute(field2, "pt", CHIP_SWAP)
    column = jnp.concatenate([jnp.where(chip == 0, field2, other), jnp.where(chip == 0, other, field2)], axis=0)
    other = lax.ppermute(column, "pt", CORE_SWAP)
    return jnp.concatenate([jnp.where(core == 0, column, other), jnp.where(core == 0, other, column)], axis=1)


def solution(mesh):
    placed = (P("slab", None), P("slab"), P("slab", "pt"), P(None, "slab", None), P())
    return jax.shard_map(
        body, mesh=mesh, in_specs=placed, out_specs=P("slab", None), check_vma=False
    )
```

```python
import jax
import jax.numpy as jnp
import numpy as np
from jax import lax
from jax.experimental import pallas as pl
from jax.experimental.pallas import tpu as pltpu
from jax.sharding import PartitionSpec as P


NB = 256
HALF = 128
NY = 8
NX = 32
PLANE = NY * NX
ROWS = 2048
SHARE = 1024
PTS = 2048
CAP = 64
ALL = 4 * CAP
WIN = 272
TILE = 256
BF = jnp.bfloat16
F32 = jnp.float32

stencil_coef = (-205.0 / 72.0, 8.0 / 5.0, -1.0 / 5.0, 8.0 / 315.0, -1.0 / 560.0)


def slab_id(y, x, z):
    return ((y % 4) * 4 + (x % 4)) * 4 + (z % 4)


def z_shift(d):
    return [(slab_id(y, x, z), slab_id(y, x, z - d)) for y in range(4) for x in range(4) for z in range(4)]


def plane_shift(d, second):
    pairs = []
    for y in range(4):
        for x in range(4):
            for z in range(4):
                for p in range(4):
                    along_x = (p % 2 == 0) != second
                    target = slab_id(y, x - d, z) if along_x else slab_id(y - d, x, z)
                    pairs.append((slab_id(y, x, z) * 4 + p, target * 4 + p))
    return pairs


BOTH = ("slab", "pt")
CORE_SWAP = [(i, i ^ 1) for i in range(4)]
CHIP_SWAP = [(i, i ^ 2) for i in range(4)]
EDGE_SWAP = [(s * 4 + 2 + c, ((s + 1) % 64) * 4 + c) for s in range(64) for c in range(2)] + [
    (s * 4 + c, ((s - 1) % 64) * 4 + 2 + c) for s in range(64) for c in range(2)
]


def plane_table():
    cell_ids = np.arange(PLANE)
    row_y = cell_ids // NX
    col_x = cell_ids % NX
    diff_y = (row_y[:, None] - row_y[None, :]) % NY
    diff_x = (col_x[:, None] - col_x[None, :]) % NX
    same_y = row_y[:, None] == row_y[None, :]
    same_x = col_x[:, None] == col_x[None, :]
    table = np.zeros((PLANE, PLANE), np.float32)
    for offset in range(1, 5):
        coef = np.float32(stencil_coef[offset])
        table += coef * (same_y & (diff_x == offset % NX)) + coef * (same_y & (diff_x == -offset % NX))
        table += coef * (same_x & (diff_y == offset % NY)) + coef * (same_x & (diff_y == -offset % NY))
    return table


def split_table():
    table = jnp.asarray(plane_table())
    high = table.astype(BF)
    low = (table - high.astype(F32)).astype(BF)
    return jnp.concatenate([high, low], axis=0)


VMEM = pl.BlockSpec(memory_space=pltpu.VMEM)


def near(value):
    return pltpu.with_memory_space_constraint(value, pltpu.VMEM)


def call(kernel, scalars, args, specs, out_shape, out_specs=None, grid=(1,), scratch=(), aliases=None):
    if out_specs is None:
        out_specs = [VMEM] * len(out_shape)
    args = [near(a) if spec is VMEM else a for a, spec in zip(args, specs)]
    out_shape = [pltpu.VMEM(o.shape, o.dtype) if spec is VMEM else o for o, spec in zip(out_shape, out_specs)]
    return pl.pallas_call(
        kernel,
        grid_spec=pltpu.PrefetchScalarGridSpec(
            num_scalar_prefetch=1, grid=grid, in_specs=specs, out_specs=out_specs, scratch_shapes=list(scratch)
        ),
        out_shape=out_shape,
        input_output_aliases=aliases or {},
        compiler_params=pltpu.CompilerParams(vmem_limit_bytes=16 << 20),
    )(scalars, *args)


def array(shape, kind):
    return jax.ShapeDtypeStruct(shape, kind)


def as_column(row):
    size = row.shape[1]
    diag = lax.broadcasted_iota(jnp.int32, (size, size), 0) == lax.broadcasted_iota(jnp.int32, (size, size), 1)
    spread = jnp.broadcast_to(row.astype(F32), (size, size))
    return jnp.sum(jnp.where(diag, spread, 0.0), axis=1, keepdims=True).astype(jnp.int32)


def selection(column, start, width):
    lanes = lax.broadcasted_iota(jnp.int32, (column.shape[0], width), 1) + start
    return jnp.where(column == lanes, 1.0, 0.0).astype(BF)


def all_columns(rows_ref):
    return jnp.concatenate([as_column(rows_ref[p]) for p in range(4)], axis=0)


def pick_own_kernel(meta_ref, rows_ref, field_ref, out_ref):
    hot = selection(as_column(rows_ref[0]), 0, ROWS)
    out_ref[...] = jnp.dot(hot, field_ref[...], preferred_element_type=F32).astype(BF)


def pick_own(meta, rows, field):
    return call(
        pick_own_kernel, meta, (rows, field),
        [pl.BlockSpec((1, 1, CAP), lambda i, m: (m[0], 0, 0)), pl.BlockSpec((ROWS, NB), lambda i, m: (0, 0))],
        [array((CAP, NB), BF)],
    )[0]


def pick_all_kernel(meta_ref, rows_ref, field_ref, fit_ref, orb_out, fit_out, hot_ref):
    @pl.when(pl.program_id(0) == 0)
    def _():
        hot_ref[...] = selection(all_columns(rows_ref), 0, ROWS)
        orb_out[...] = jnp.dot(hot_ref[...], field_ref[...], preferred_element_type=F32).astype(BF)

    fit_out[...] = jnp.dot(hot_ref[...], fit_ref[...], preferred_element_type=F32).astype(BF)


def pick_all(meta, rows, field, fit):
    return call(
        pick_all_kernel, meta, (rows, field, fit),
        [VMEM, VMEM, pl.BlockSpec((ROWS, 512), lambda i, m: (0, i))],
        [array((ALL, NB), BF), array((ALL, PTS), BF)],
        [pl.BlockSpec((ALL, NB), lambda i, m: (0, 0)), pl.BlockSpec((ALL, 512), lambda i, m: (0, i))],
        grid=(4,), scratch=[pltpu.VMEM((ALL, ROWS), BF)],
    )


def stencil_kernel(meta_ref, rows_ref, own_ref, inner_ref, outer_ref, pot_ref, table_ref, local_ref, *picked):
    first = meta_ref[2] == 0
    planes = []
    for k in range(4):
        part = pl.ds(k * PLANE, PLANE)
        planes.append(jnp.where(first, outer_ref[part, :], inner_ref[part, :]).astype(F32))
    planes += [own_ref[pl.ds(k * PLANE, PLANE), :].astype(F32) for k in range(4)]
    for k in range(4):
        part = pl.ds(k * PLANE, PLANE)
        planes.append(jnp.where(first, inner_ref[part, :], outer_ref[part, :]).astype(F32))
    for k in range(4):
        part = pl.ds(k * PLANE, PLANE)
        own = own_ref[part, :]
        center = planes[4 + k]
        total = jnp.dot(table_ref[pl.ds(0, PLANE), :], own, preferred_element_type=F32)
        total += jnp.dot(table_ref[pl.ds(PLANE, PLANE), :], own, preferred_element_type=F32)
        total += 3.0 * stencil_coef[0] * center
        for offset in range(1, 5):
            total += stencil_coef[offset] * (planes[4 + k + offset] + planes[4 + k - offset])
        local_ref[part, :] = -0.5 * total + pot_ref[part, :] * center
    if picked:
        hot = selection(all_columns(rows_ref), meta_ref[2] * SHARE, SHARE)
        picked[0][...] = jnp.dot(hot, local_ref[...].astype(BF), preferred_element_type=F32)


def stencil(meta, rows, own, inner, outer, potential, table, with_pick):
    shapes = [array((SHARE, HALF), F32)]
    if with_pick:
        shapes.append(array((ALL, HALF), F32))
    return call(stencil_kernel, meta, (rows, own, inner, outer, potential, table), [VMEM] * 6, shapes)


def place(meta_ref, where_ref, sum_ref, group, rows):
    line = lax.broadcasted_iota(jnp.int32, (WIN, TILE), 0)
    hot = jnp.where(where_ref[group : group + 1, :] == line, 1.0, 0.0).astype(BF)
    at = pl.multiple_of(meta_ref[4 + group], 8)
    sum_ref[pl.ds(at, WIN), :] += jnp.dot(hot, rows, preferred_element_type=F32)


def place_early_kernel(meta_ref, where_ref, line_ref, up_ref, down_ref, sum_ref):
    sum_ref[...] = jnp.zeros_like(sum_ref)
    for part, ref in ((0, line_ref), (1, up_ref), (3, down_ref)):
        for e in range(4):
            place(meta_ref, where_ref, sum_ref, part * 4 + e, ref[pl.ds(e * TILE, TILE), :])


def place_early(meta, where, line, up, down):
    return call(place_early_kernel, meta, (where, line, up, down), [VMEM] * 4, [array((PTS + WIN, NB), F32)])[0]


def place_late(meta_ref, where_ref, left_ref, right_ref, sum_ref, psi_ref):
    for e in range(4):
        ref = left_ref if e < 2 else right_ref
        place(meta_ref, where_ref, sum_ref, 8 + e, ref[pl.ds((e % 2) * TILE, TILE), :])
    psi_ref[...] = sum_ref[pl.ds(0, PTS), :].astype(BF)


def place_late_kernel(meta_ref, where_ref, left_ref, right_ref, early_ref, sum_ref, psi_ref):
    place_late(meta_ref, where_ref, left_ref, right_ref, sum_ref, psi_ref)


def listed_kernel(meta_ref, where_ref, left_ref, right_ref, early_ref, orb_ref, fit_ref, local_ref,
                  sum_ref, psi_ref, pick_ref):
    place_late(meta_ref, where_ref, left_ref, right_ref, sum_ref, psi_ref)
    density = lax.dot_general(orb_ref[...], psi_ref[...], (((1,), (1,)), ((), ())), preferred_element_type=F32)
    kern = (fit_ref[...].astype(F32) * density).astype(BF)
    part = -jnp.dot(kern, psi_ref[...], preferred_element_type=F32)
    core = meta_ref[1]
    local = local_ref[...]
    pick_ref[:, :HALF] = (part[:, :HALF] + jnp.where(core == 0, local, 0.0)).astype(BF)
    pick_ref[:, HALF:] = (part[:, HALF:] + jnp.where(core == 0, 0.0, local)).astype(BF)


def listed(meta, where, left, right, early, orb, fit, local):
    return call(
        listed_kernel, meta, (where, left, right, early, orb, fit, local), [VMEM] * 7,
        [array((PTS + WIN, NB), F32), array((PTS, NB), BF), array((ALL, NB), BF)], aliases={4: 0},
    )[1:]


def finish_points(meta, where, left, right, early):
    return call(
        place_late_kernel, meta, (where, left, right, early), [VMEM] * 4,
        [array((PTS + WIN, NB), F32), array((PTS, NB), BF)], aliases={4: 0},
    )[1]


def emit(meta_ref, part, keep_ref, send_ref, at):
    core = meta_ref[1]
    left, right = part[:, :HALF], part[:, HALF:]
    keep_ref[at, :] = jnp.where(core == 0, left, right)
    send_ref[at, :] = jnp.where(core == 0, right, left).astype(BF)


def build_kernel(meta_ref, psi_ref, orb_ref, fit_ref, kern_ref, keep_ref, send_ref):
    at = pl.ds(pl.multiple_of(pl.program_id(0) * TILE, TILE), TILE)
    density = lax.dot_general(orb_ref[...], psi_ref[...], (((1,), (1,)), ((), ())), preferred_element_type=F32)
    kern = (fit_ref[...].astype(F32) * density).astype(BF)
    kern_ref[at, :] = kern
    emit(meta_ref, -jnp.dot(kern, psi_ref[...], preferred_element_type=F32), keep_ref, send_ref, at)


def build(meta, psi, orb, fit, away):
    def mapped(i, m):
        return (i + 4 * (1 - m[2] if away else m[2]), 0)

    return call(
        build_kernel, meta, (psi, orb, fit),
        [VMEM, pl.BlockSpec((TILE, NB), mapped), pl.BlockSpec((TILE, PTS), mapped)],
        [array((SHARE, PTS), BF), array((SHARE, HALF), F32), array((SHARE, HALF), BF)], grid=(4,),
    )


def apply_kernel(meta_ref, psi_ref, kern_ref, keep_ref, send_ref):
    for step in range(4):
        at = pl.ds(step * TILE, TILE)
        part = -jnp.dot(kern_ref[at, :], psi_ref[...], preferred_element_type=F32)
        emit(meta_ref, part, keep_ref, send_ref, at)


def apply(meta, psi, kern):
    return call(
        apply_kernel, meta, (psi, kern), [VMEM, VMEM],
        [array((SHARE, HALF), F32), array((SHARE, HALF), BF)],
    )


def after(value, *earlier):
    return lax.optimization_barrier((value,) + earlier)[0]


def gather_column(own):
    parts = [own] + [lax.ppermute(own, "slab", z_shift(d)) for d in (1, 2, 3)]
    return jnp.concatenate(parts, axis=0)


def gather_line(column):
    parts = [column] + [lax.ppermute(column, BOTH, plane_shift(d, False)) for d in (1, 2, 3)]
    return jnp.concatenate(parts, axis=0)


def gather_sides(line):
    return (lax.ppermute(line, BOTH, plane_shift(1, True)), lax.ppermute(line, BOTH, plane_shift(-1, True)))


def gather_far(up, down):
    left = lax.ppermute(up[: 2 * TILE], BOTH, plane_shift(1, True))
    right = lax.ppermute(down[2 * TILE :], BOTH, plane_shift(-1, True))
    return left, right


def body(orbitals, potential, fit_matrix, owner_rows, owner_count):
    point_block = lax.axis_index("pt")
    slab = lax.axis_index("slab")
    core = point_block % 2
    chip = point_block // 2
    my_z = slab % 4
    my_x = (slab // 4) % 4
    my_y = slab // 16

    counts = lax.dynamic_index_in_dim(owner_count, point_block, 0, keepdims=False)
    four = jnp.arange(4, dtype=jnp.int32)
    outer_step = four[:, None, None]
    inner_step = four[None, :, None]
    y_id = jnp.where(core == 0, my_y + outer_step, my_y + inner_step) % 4
    x_id = jnp.where(core == 0, my_x + inner_step, my_x + outer_step) % 4
    z_id = (my_z + four[None, None, :]) % 4
    column_id = y_id * 4 + x_id
    slabs = (column_id * 4 + z_id).reshape(16, 4)
    first = (column_id * 4).reshape(16)
    every = jnp.arange(64, dtype=jnp.int32)
    start = jnp.sum(jnp.where(every < slabs[:, :, None], counts, 0), axis=2)
    size = jnp.sum(jnp.where(every == slabs[:, :, None], counts, 0), axis=2)
    base = jnp.sum(jnp.where(every[None, :] < first[:, None], counts, 0), axis=1) // 8 * 8
    slot = jnp.arange(CAP, dtype=jnp.int32)
    where = jnp.where(slot < size[:, :, None], start[:, :, None] - base[:, None, None] + slot, -1).reshape(16, TILE)
    ids = jnp.stack([point_block, core, chip, slab]).astype(jnp.int32)
    meta = jnp.concatenate([ids, base.astype(jnp.int32)])
    table = split_table()
    row0 = chip * SHARE

    own0 = pick_own(ids, owner_rows, orbitals)
    column0 = gather_column(own0)
    line0 = gather_line(column0)
    up0, down0 = gather_sides(line0)
    left0, right0 = gather_far(up0, down0)

    field0 = lax.dynamic_slice(orbitals, (row0, core * HALF), (SHARE, HALF))
    inner0 = lax.dynamic_slice(orbitals, (SHARE - row0, core * HALF), (SHARE, HALF))
    potential_piece = lax.dynamic_slice(potential, (row0,), (SHARE,)).reshape(SHARE, 1)
    outer0 = lax.ppermute(after(field0, column0), BOTH, EDGE_SWAP)
    orb_listed, fit_listed = pick_all(ids, after(owner_rows, column0), orbitals, fit_matrix)
    local0, local_listed = stencil(ids, owner_rows, field0, inner0, outer0, potential_piece, table, True)

    early0 = place_early(meta, where, line0, up0, down0)
    psi0, picked = listed(meta, where, left0, right0, early0, orb_listed, fit_listed, local_listed)

    pieces = lax.all_to_all(picked.reshape(4, CAP, NB), "pt", 0, 0)
    applied = jnp.sum(pieces.astype(F32), axis=0)
    own1 = ((applied - 3.5 * own0.astype(F32)) / 4.0).astype(BF)
    column1 = gather_column(own1)
    line1 = gather_line(column1)
    up1, down1 = gather_sides(line1)
    left1, right1 = gather_far(up1, down1)

    def send_away(keep, gone):
        total = keep + lax.ppermute(gone, "pt", CORE_SWAP).astype(F32)
        return lax.ppermute(total.astype(BF), "pt", CHIP_SWAP)

    def join_own(keep, gone, away):
        return keep + lax.ppermute(gone, "pt", CORE_SWAP).astype(F32) + away.astype(F32)

    kern_away, keep, gone = build(meta, after(psi0, own1), orbitals, fit_matrix, True)
    away = send_away(keep, gone)
    kern_own, keep, gone = build(meta, after(psi0, column1), orbitals, fit_matrix, False)
    applied0 = local0 + join_own(keep, gone, away)
    field1 = ((applied0 - 3.5 * field0.astype(F32)) / 4.0).astype(BF)
    inner1 = lax.ppermute(field1, "pt", CHIP_SWAP)
    outer1 = lax.ppermute(field1, BOTH, EDGE_SWAP)
    local1 = stencil(ids, owner_rows, field1, inner1, outer1, potential_piece, table, False)[0]

    early1 = place_early(meta, where, line1, up1, down1)
    psi1 = finish_points(meta, where, left1, right1, early1)
    keep, gone = apply(meta, psi1, kern_away)
    away = send_away(keep, gone)
    keep, gone = apply(meta, after(psi1, keep), kern_own)
    applied1 = local1 + join_own(keep, gone, away)
    field2 = (0.5 * (applied1 - 3.5 * field1.astype(F32)) - field0.astype(F32)).astype(BF)

    other = lax.ppermute(field2, "pt", CHIP_SWAP)
    column = jnp.concatenate([jnp.where(chip == 0, field2, other), jnp.where(chip == 0, other, field2)], axis=0)
    other = lax.ppermute(column, "pt", CORE_SWAP)
    return jnp.concatenate([jnp.where(core == 0, column, other), jnp.where(core == 0, other, column)], axis=1)


def solution(mesh):
    placed = (P("slab", None), P("slab"), P("slab", "pt"), P(None, "slab", None), P())
    return jax.shard_map(body, mesh=mesh, in_specs=placed, out_specs=P("slab", None), check_vma=False)
```

```python
import jax
import jax.numpy as jnp
import numpy as np
from jax import lax
from jax.experimental import pallas as pl
from jax.experimental.pallas import tpu as pltpu
from jax.sharding import PartitionSpec as P


NB = 256
HALF = 128
NY = 8
NX = 32
PLANE = NY * NX
ROWS = 2048
SHARE = 1024
PTS = 2048
CAP = 64
ALL = 4 * CAP
WIN = 272
TILE = 256
BF = jnp.bfloat16
F32 = jnp.float32

stencil_coef = (-205.0 / 72.0, 8.0 / 5.0, -1.0 / 5.0, 8.0 / 315.0, -1.0 / 560.0)


def slab_id(y, x, z):
    return ((y % 4) * 4 + (x % 4)) * 4 + (z % 4)


def z_shift(d):
    return [(slab_id(y, x, z), slab_id(y, x, z - d)) for y in range(4) for x in range(4) for z in range(4)]


def plane_shift(d, second):
    pairs = []
    for y in range(4):
        for x in range(4):
            for z in range(4):
                for p in range(4):
                    along_x = (p % 2 == 0) != second
                    target = slab_id(y, x - d, z) if along_x else slab_id(y - d, x, z)
                    pairs.append((slab_id(y, x, z) * 4 + p, target * 4 + p))
    return pairs


BOTH = ("slab", "pt")
CORE_SWAP = [(i, i ^ 1) for i in range(4)]
CHIP_SWAP = [(i, i ^ 2) for i in range(4)]
EDGE_SWAP = [(s * 4 + 2 + c, ((s + 1) % 64) * 4 + c) for s in range(64) for c in range(2)] + [
    (s * 4 + c, ((s - 1) % 64) * 4 + 2 + c) for s in range(64) for c in range(2)
]


def plane_table():
    cell_ids = np.arange(PLANE)
    row_y = cell_ids // NX
    col_x = cell_ids % NX
    diff_y = (row_y[:, None] - row_y[None, :]) % NY
    diff_x = (col_x[:, None] - col_x[None, :]) % NX
    same_y = row_y[:, None] == row_y[None, :]
    same_x = col_x[:, None] == col_x[None, :]
    table = np.zeros((PLANE, PLANE), np.float32)
    for offset in range(1, 5):
        coef = np.float32(stencil_coef[offset])
        table += coef * (same_y & (diff_x == offset % NX)) + coef * (same_y & (diff_x == -offset % NX))
        table += coef * (same_x & (diff_y == offset % NY)) + coef * (same_x & (diff_y == -offset % NY))
    return table


def split_table():
    table = jnp.asarray(plane_table())
    high = table.astype(BF)
    low = (table - high.astype(F32)).astype(BF)
    return jnp.concatenate([high, low], axis=0)


VMEM = pl.BlockSpec(memory_space=pltpu.VMEM)
HBM = pl.BlockSpec(memory_space=pltpu.HBM)


def near(value):
    return pltpu.with_memory_space_constraint(value, pltpu.VMEM)


def far_away(value):
    return pltpu.with_memory_space_constraint(value, pltpu.HBM)


def call(kernel, scalars, args, specs, out_shape, out_specs=None, grid=(1,), scratch=(), aliases=None):
    if out_specs is None:
        out_specs = [VMEM] * len(out_shape)
    args = [near(a) if spec is VMEM else far_away(a) if spec is HBM else a for a, spec in zip(args, specs)]
    out_shape = [pltpu.VMEM(o.shape, o.dtype) if spec is VMEM else o for o, spec in zip(out_shape, out_specs)]
    return pl.pallas_call(
        kernel,
        grid_spec=pltpu.PrefetchScalarGridSpec(
            num_scalar_prefetch=1, grid=grid, in_specs=specs, out_specs=out_specs, scratch_shapes=list(scratch)
        ),
        out_shape=out_shape,
        input_output_aliases=aliases or {},
        compiler_params=pltpu.CompilerParams(vmem_limit_bytes=16 << 20),
    )(scalars, *args)


def array(shape, kind):
    return jax.ShapeDtypeStruct(shape, kind)


def as_column(row):
    size = row.shape[1]
    diag = lax.broadcasted_iota(jnp.int32, (size, size), 0) == lax.broadcasted_iota(jnp.int32, (size, size), 1)
    spread = jnp.broadcast_to(row.astype(F32), (size, size))
    return jnp.sum(jnp.where(diag, spread, 0.0), axis=1, keepdims=True).astype(row.dtype)


def selection(column, start, width):
    lanes = lax.broadcasted_iota(jnp.int32, (column.shape[0], width), 1) + start
    return jnp.where(column == lanes, 1.0, 0.0).astype(BF)


def all_columns(rows_ref):
    return jnp.concatenate([as_column(rows_ref[p]) for p in range(4)], axis=0)


def index_kernel(ids_ref, count_ref, where_ref, meta_ref, start_ref):
    block, core, slab = ids_ref[0], ids_ref[1], ids_ref[3]
    my_y, my_x, my_z = slab // 16, (slab // 4) % 4, slab % 4
    start_ref[0] = 0

    def add(n, carry):
        start_ref[n + 1] = start_ref[n] + count_ref[block, n]
        return carry

    lax.fori_loop(0, 64, add, 0)
    for n in range(4):
        meta_ref[n] = ids_ref[n]
    lane = lax.broadcasted_iota(jnp.int32, (1, TILE), 1)
    for outer in range(4):
        for inner in range(4):
            y_step, x_step = jnp.where(core == 0, outer, inner), jnp.where(core == 0, inner, outer)
            first = (((my_y + y_step) % 4) * 4 + (my_x + x_step) % 4) * 4
            base = start_ref[first] // 8 * 8
            meta_ref[4 + outer * 4 + inner] = base
            row = jnp.full((1, TILE), -1, jnp.int32)
            for d in range(4):
                slab_d = first + (my_z + d) % 4
                begin = start_ref[slab_d]
                size = start_ref[slab_d + 1] - begin
                slot = lane - d * CAP
                row = jnp.where((slot >= 0) & (slot < size), begin - base + slot, row)
            where_ref[pl.ds(outer * 4 + inner, 1), :] = row


def index(ids, counts):
    smem = pl.BlockSpec(memory_space=pltpu.SMEM)
    return call(
        index_kernel, ids, (counts,), [smem], [array((16, TILE), jnp.int32), array((20,), jnp.int32)],
        [VMEM, smem], scratch=[pltpu.SMEM((72,), jnp.int32)],
    )


def pick_own_kernel(meta_ref, rows_ref, field_ref, out_ref):
    hot = selection(as_column(rows_ref[0]), 0, ROWS)
    out_ref[...] = jnp.dot(hot, field_ref[...], preferred_element_type=F32).astype(BF)


def pick_own(meta, rows, field):
    return call(
        pick_own_kernel, meta, (rows, field),
        [pl.BlockSpec((1, 1, CAP), lambda i, m: (m[0], 0, 0)), pl.BlockSpec((ROWS, NB), lambda i, m: (0, 0))],
        [array((CAP, NB), BF)],
    )[0]


def pick_all_kernel(meta_ref, rows_ref, field_ref, fit_ref, orb_out, fit_out, hot_ref):
    @pl.when(pl.program_id(0) == 0)
    def _():
        hot_ref[...] = selection(all_columns(rows_ref), 0, ROWS)
        orb_out[...] = jnp.dot(hot_ref[...], field_ref[...], preferred_element_type=F32).astype(BF)

    at = pl.ds(pl.multiple_of(pl.program_id(0) * 512, 512), 512)
    fit_out[:, at] = jnp.dot(hot_ref[...], fit_ref[:, at], preferred_element_type=F32).astype(BF)


def pick_all(meta, rows, field, fit):
    return call(
        pick_all_kernel, meta, (rows, field, fit), [VMEM] * 3,
        [array((ALL, NB), BF), array((ALL, PTS), BF)], grid=(4,), scratch=[pltpu.VMEM((ALL, ROWS), BF)],
    )


def stencil_kernel(meta_ref, rows_ref, own_ref, inner_ref, outer_ref, pot_ref, table_ref, local_ref, *picked):
    first = meta_ref[2] == 0
    pot = pot_ref[pl.ds(pl.multiple_of(meta_ref[2] * 8, 8), 8), :]
    planes = []
    for k in range(4):
        part = pl.ds(k * PLANE, PLANE)
        planes.append(jnp.where(first, outer_ref[part, :], inner_ref[part, :]).astype(F32))
    planes += [own_ref[pl.ds(k * PLANE, PLANE), :].astype(F32) for k in range(4)]
    for k in range(4):
        part = pl.ds(k * PLANE, PLANE)
        planes.append(jnp.where(first, inner_ref[part, :], outer_ref[part, :]).astype(F32))
    for k in range(4):
        part = pl.ds(k * PLANE, PLANE)
        own = own_ref[part, :]
        center = planes[4 + k]
        total = jnp.dot(table_ref[pl.ds(0, PLANE), :], own, preferred_element_type=F32)
        total += jnp.dot(table_ref[pl.ds(PLANE, PLANE), :], own, preferred_element_type=F32)
        total += 3.0 * stencil_coef[0] * center
        for offset in range(1, 5):
            total += stencil_coef[offset] * (planes[4 + k + offset] + planes[4 + k - offset])
        scale = jnp.concatenate([as_column(pot[2 * k + n : 2 * k + n + 1, :]) for n in (0, 1)], axis=0)
        local_ref[part, :] = -0.5 * total + scale * center
    if picked:
        hot = selection(all_columns(rows_ref), meta_ref[2] * SHARE, SHARE)
        picked[0][...] = jnp.dot(hot, local_ref[...].astype(BF), preferred_element_type=F32)


def stencil(meta, rows, own, inner, outer, potential, table, with_pick):
    shapes = [array((SHARE, HALF), F32)]
    if with_pick:
        shapes.append(array((ALL, HALF), F32))
    return call(stencil_kernel, meta, (rows, own, inner, outer, potential, table), [VMEM] * 6, shapes)


def place(meta_ref, where_ref, sum_ref, group, rows):
    line = lax.broadcasted_iota(jnp.int32, (WIN, TILE), 0)
    hot = jnp.where(where_ref[group : group + 1, :] == line, 1.0, 0.0).astype(BF)
    at = pl.multiple_of(meta_ref[4 + group], 8)
    sum_ref[pl.ds(at, WIN), :] += jnp.dot(hot, rows, preferred_element_type=F32)


def place_early_kernel(meta_ref, where_ref, line_ref, up_ref, down_ref, sum_ref):
    sum_ref[...] = jnp.zeros_like(sum_ref)
    for part, ref in ((0, line_ref), (1, up_ref), (3, down_ref)):
        for e in range(4):
            place(meta_ref, where_ref, sum_ref, part * 4 + e, ref[pl.ds(e * TILE, TILE), :])


def place_early(meta, where, line, up, down):
    return call(place_early_kernel, meta, (where, line, up, down), [VMEM] * 4, [array((PTS + WIN, NB), F32)])[0]


def place_late(meta_ref, where_ref, left_ref, right_ref, sum_ref, psi_ref):
    for e in range(4):
        ref = left_ref if e < 2 else right_ref
        place(meta_ref, where_ref, sum_ref, 8 + e, ref[pl.ds((e % 2) * TILE, TILE), :])
    psi_ref[...] = sum_ref[pl.ds(0, PTS), :].astype(BF)


def place_late_kernel(meta_ref, where_ref, left_ref, right_ref, early_ref, sum_ref, psi_ref):
    place_late(meta_ref, where_ref, left_ref, right_ref, sum_ref, psi_ref)


def listed_kernel(meta_ref, where_ref, left_ref, right_ref, early_ref, orb_ref, fit_ref, local_ref,
                  sum_ref, psi_ref, keep_ref, gone_ref):
    place_late(meta_ref, where_ref, left_ref, right_ref, sum_ref, psi_ref)
    density = lax.dot_general(orb_ref[...], psi_ref[...], (((1,), (1,)), ((), ())), preferred_element_type=F32)
    kern = (fit_ref[...].astype(F32) * density).astype(BF)
    part = -jnp.dot(kern, psi_ref[...], preferred_element_type=F32)
    core = meta_ref[1]
    first = meta_ref[2] == 0
    local = local_ref[...]
    part = jnp.concatenate(
        [part[:, :HALF] + jnp.where(core == 0, local, 0.0), part[:, HALF:] + jnp.where(core == 0, 0.0, local)], axis=1
    )
    mine = [jnp.where(core == 0, part[c * 128 : c * 128 + CAP], part[c * 128 + CAP : c * 128 + 128]) for c in (0, 1)]
    other = [jnp.where(core == 0, part[c * 128 + CAP : c * 128 + 128], part[c * 128 : c * 128 + CAP]) for c in (0, 1)]
    keep_ref[:CAP, :] = jnp.where(first, mine[0], mine[1])
    keep_ref[CAP:, :] = jnp.where(first, mine[1], mine[0])
    gone_ref[:CAP, :] = jnp.where(first, other[0], other[1]).astype(BF)
    gone_ref[CAP:, :] = jnp.where(first, other[1], other[0]).astype(BF)


def listed(meta, where, left, right, early, orb, fit, local):
    return call(
        listed_kernel, meta, (where, left, right, early, orb, fit, local), [VMEM] * 7,
        [array((PTS + WIN, NB), F32), array((PTS, NB), BF), array((2 * CAP, NB), F32), array((2 * CAP, NB), BF)],
        aliases={4: 0},
    )[1:]


def pair_kernel(meta_ref, keep_ref, got_ref, near_ref, far_ref):
    near_ref[...] = keep_ref[:CAP, :] + got_ref[:CAP, :].astype(F32)
    far_ref[...] = (keep_ref[CAP:, :] + got_ref[CAP:, :].astype(F32)).astype(BF)


def pair_up(meta, keep, got):
    return call(pair_kernel, meta, (keep, got), [VMEM] * 2, [array((CAP, NB), F32), array((CAP, NB), BF)])


def update_kernel(meta_ref, near_ref, far_ref, old_ref, new_ref):
    applied = near_ref[...] + far_ref[...].astype(F32)
    new_ref[...] = ((applied - 3.5 * old_ref[...].astype(F32)) / 4.0).astype(BF)


def update_points(meta, near_part, far_part, old):
    return call(update_kernel, meta, (near_part, far_part, old), [VMEM] * 3, [array((CAP, NB), BF)])[0]


def stage_kernel(meta_ref, fit_ref, out_ref, sem):
    copy = pltpu.make_async_copy(fit_ref, out_ref, sem)
    copy.start()
    copy.wait()


def stage(meta, fit):
    return call(
        stage_kernel, meta, (fit,), [HBM], [array((ROWS, PTS), BF)],
        scratch=[pltpu.SemaphoreType.DMA],
    )[0]


def join_kernel(meta_ref, *refs):
    size = refs[0].shape[0]
    for n, ref in enumerate(refs[:-1]):
        refs[-1][pl.ds(n * size, size), :] = ref[...]


def join(meta, parts):
    shape = (len(parts) * parts[0].shape[0], NB)
    return call(join_kernel, meta, parts, [VMEM] * len(parts), [array(shape, BF)])[0]


def halves_kernel(meta_ref, up_ref, down_ref, left_ref, right_ref):
    left_ref[...] = up_ref[: 2 * TILE, :]
    right_ref[...] = down_ref[2 * TILE :, :]


def halves(meta, up, down):
    return call(halves_kernel, meta, (up, down), [VMEM] * 2, [array((2 * TILE, NB), BF)] * 2)


def finish_points(meta, where, left, right, early):
    return call(
        place_late_kernel, meta, (where, left, right, early), [VMEM] * 4,
        [array((PTS + WIN, NB), F32), array((PTS, NB), BF)], aliases={4: 0},
    )[1]


def emit(meta_ref, part, keep_ref, send_ref, at):
    core = meta_ref[1]
    left, right = part[:, :HALF], part[:, HALF:]
    keep_ref[at, :] = jnp.where(core == 0, left, right)
    send_ref[at, :] = jnp.where(core == 0, right, left).astype(BF)


def build_with(away):
    def build_kernel(meta_ref, psi_ref, orb_ref, fit_ref, kern_ref, keep_ref, send_ref):
        step = pl.program_id(0)
        half = 1 - meta_ref[2] if away else meta_ref[2]
        at = pl.ds(pl.multiple_of(step * TILE, TILE), TILE)
        rows = pl.ds(pl.multiple_of(half * SHARE + step * TILE, TILE), TILE)
        density = lax.dot_general(
            orb_ref[rows, :], psi_ref[...], (((1,), (1,)), ((), ())), preferred_element_type=F32
        )
        kern = (fit_ref[rows, :].astype(F32) * density).astype(BF)
        kern_ref[at, :] = kern
        emit(meta_ref, -jnp.dot(kern, psi_ref[...], preferred_element_type=F32), keep_ref, send_ref, at)

    return build_kernel


def build(meta, psi, orb, fit, away):
    return call(
        build_with(away), meta, (psi, orb, fit), [VMEM] * 3,
        [array((SHARE, PTS), BF), array((SHARE, HALF), F32), array((SHARE, HALF), BF)], grid=(4,),
    )


def apply_kernel(meta_ref, psi_ref, kern_ref, keep_ref, send_ref):
    for step in range(4):
        at = pl.ds(step * TILE, TILE)
        part = -jnp.dot(kern_ref[at, :], psi_ref[...], preferred_element_type=F32)
        emit(meta_ref, part, keep_ref, send_ref, at)


def apply(meta, psi, kern):
    return call(
        apply_kernel, meta, (psi, kern), [VMEM, VMEM],
        [array((SHARE, HALF), F32), array((SHARE, HALF), BF)],
    )


def sum_kernel(meta_ref, keep_ref, got_ref, sum_ref):
    sum_ref[...] = (keep_ref[...] + got_ref[...].astype(F32)).astype(BF)


def sum_away(meta, keep, got):
    return call(sum_kernel, meta, (keep, got), [VMEM] * 2, [array((SHARE, HALF), BF)])[0]


def field_kernel(meta_ref, local_ref, keep_ref, core_ref, chip_ref, field_ref, *rest):
    current = field_ref[...].astype(F32)
    applied = local_ref[...] + (keep_ref[...] + core_ref[...].astype(F32) + chip_ref[...].astype(F32))
    scaled = applied - 3.5 * current
    if len(rest) == 1:
        rest[0][...] = (scaled / 4.0).astype(BF)
    else:
        rest[1][...] = (0.5 * scaled - rest[0][...].astype(F32)).astype(BF)


def next_field(meta, local, parts, *fields):
    return call(
        field_kernel, meta, (local, *parts, *fields), [VMEM] * (4 + len(fields)),
        [array((SHARE, HALF), BF)],
    )[0]


def after(value, *earlier):
    return lax.optimization_barrier((value,) + earlier)[0]


def gather_column(meta, own):
    parts = [own] + [lax.ppermute(own, "slab", z_shift(d)) for d in (1, 2, 3)]
    return join(meta, parts)


def gather_line(meta, column):
    parts = [column] + [lax.ppermute(column, BOTH, plane_shift(d, False)) for d in (1, 2, 3)]
    return join(meta, parts)


def gather_sides(line):
    return (lax.ppermute(line, BOTH, plane_shift(1, True)), lax.ppermute(line, BOTH, plane_shift(-1, True)))


def gather_far(meta, up, down):
    near_up, near_down = halves(meta, up, down)
    left = lax.ppermute(near_up, BOTH, plane_shift(1, True))
    right = lax.ppermute(near_down, BOTH, plane_shift(-1, True))
    return left, right


def body(orbitals, potential, fit_matrix, owner_rows, owner_count):
    point_block = lax.axis_index("pt")
    slab = lax.axis_index("slab")
    core = point_block % 2
    chip = point_block // 2
    ids = jnp.stack([point_block, core, chip, slab]).astype(jnp.int32)
    table = split_table()
    row0 = chip * SHARE

    own0 = pick_own(ids, owner_rows, orbitals)
    early_orbitals = after(orbitals, own0)
    field0 = lax.dynamic_slice(early_orbitals, (row0, core * HALF), (SHARE, HALF))
    inner0 = lax.dynamic_slice(early_orbitals, (SHARE - row0, core * HALF), (SHARE, HALF))
    potential_rows = potential.reshape(16, 128)
    column0 = gather_column(ids, own0)
    fit = stage(ids, after(fit_matrix, column0, inner0))
    line0 = gather_line(ids, column0)
    up0, down0 = gather_sides(line0)
    where, meta = index(ids, after(owner_count, up0))
    left0, right0 = gather_far(ids, up0, down0)

    outer0 = lax.ppermute(field0, BOTH, EDGE_SWAP)
    orb_listed, fit_listed = pick_all(ids, after(owner_rows, line0), orbitals, fit)
    local0, local_listed = stencil(ids, owner_rows, field0, inner0, outer0, potential_rows, table, True)

    early0 = place_early(meta, where, line0, up0, down0)
    psi0, keep, gone = listed(meta, where, left0, right0, early0, orb_listed, fit_listed, local_listed)

    near_part, far_part = pair_up(ids, keep, lax.ppermute(gone, "pt", CORE_SWAP))
    other_part = lax.ppermute(far_part, "pt", CHIP_SWAP)
    own1 = update_points(ids, near_part, other_part, own0)
    column1 = gather_column(ids, own1)
    line1 = gather_line(ids, column1)
    up1, down1 = gather_sides(line1)
    left1, right1 = gather_far(ids, up1, down1)

    def send_away(keep, gone):
        total = sum_away(ids, keep, lax.ppermute(gone, "pt", CORE_SWAP))
        return lax.ppermute(total, "pt", CHIP_SWAP)

    def own_parts(keep, gone, away):
        return keep, lax.ppermute(gone, "pt", CORE_SWAP), away

    kern_away, keep, gone = build(meta, after(psi0, far_part), orbitals, fit, True)
    away = send_away(keep, gone)
    kern_own, keep, gone = build(meta, after(psi0, own1), orbitals, fit, False)
    field1 = next_field(ids, local0, own_parts(keep, gone, away), field0)
    inner1 = lax.ppermute(field1, "pt", CHIP_SWAP)
    outer1 = lax.ppermute(field1, BOTH, EDGE_SWAP)
    local1 = stencil(ids, owner_rows, field1, inner1, outer1, potential_rows, table, False)[0]

    early1 = place_early(meta, where, line1, up1, down1)
    psi1 = finish_points(meta, where, left1, right1, early1)
    keep, gone = apply(meta, psi1, kern_away)
    away = send_away(keep, gone)
    keep, gone = apply(meta, after(psi1, keep), kern_own)
    field2 = next_field(ids, local1, own_parts(keep, gone, away), field1, field0)

    other = lax.ppermute(field2, "pt", CHIP_SWAP)
    column = jnp.concatenate([jnp.where(chip == 0, field2, other), jnp.where(chip == 0, other, field2)], axis=0)
    other = lax.ppermute(column, "pt", CORE_SWAP)
    return jnp.concatenate([jnp.where(core == 0, column, other), jnp.where(core == 0, other, column)], axis=1)


def solution(mesh):
    placed = (P("slab", None), P("slab"), P("slab", "pt"), P(None, "slab", None), P())
    return jax.shard_map(body, mesh=mesh, in_specs=placed, out_specs=P("slab", None), check_vma=False)
```

```python
import jax
import jax.numpy as jnp
import numpy as np
from jax import lax
from jax.experimental import pallas as pl
from jax.experimental.pallas import tpu as pltpu
from jax.sharding import PartitionSpec as P


NB = 256
HALF = 128
NY = 8
NX = 32
PLANE = NY * NX
ROWS = 2048
SHARE = 1024
PTS = 2048
CAP = 64
ALL = 4 * CAP
WIN = 272
TILE = 256
BF = jnp.bfloat16
F32 = jnp.float32

stencil_coef = (-205.0 / 72.0, 8.0 / 5.0, -1.0 / 5.0, 8.0 / 315.0, -1.0 / 560.0)


def slab_id(y, x, z):
    return ((y % 4) * 4 + (x % 4)) * 4 + (z % 4)


def z_shift(d):
    return [(slab_id(y, x, z), slab_id(y, x, z - d)) for y in range(4) for x in range(4) for z in range(4)]


def plane_shift(d, second):
    pairs = []
    for y in range(4):
        for x in range(4):
            for z in range(4):
                for p in range(4):
                    along_x = (p % 2 == 0) != second
                    target = slab_id(y, x - d, z) if along_x else slab_id(y - d, x, z)
                    pairs.append((slab_id(y, x, z) * 4 + p, target * 4 + p))
    return pairs


BOTH = ("slab", "pt")
CORE_SWAP = [(i, i ^ 1) for i in range(4)]
CHIP_SWAP = [(i, i ^ 2) for i in range(4)]
EDGE_SWAP = [(s * 4 + 2 + c, ((s + 1) % 64) * 4 + c) for s in range(64) for c in range(2)] + [
    (s * 4 + c, ((s - 1) % 64) * 4 + 2 + c) for s in range(64) for c in range(2)
]


def plane_table():
    cell_ids = np.arange(PLANE)
    row_y = cell_ids // NX
    col_x = cell_ids % NX
    diff_y = (row_y[:, None] - row_y[None, :]) % NY
    diff_x = (col_x[:, None] - col_x[None, :]) % NX
    same_y = row_y[:, None] == row_y[None, :]
    same_x = col_x[:, None] == col_x[None, :]
    table = np.zeros((PLANE, PLANE), np.float32)
    for offset in range(1, 5):
        coef = np.float32(stencil_coef[offset])
        table += coef * (same_y & (diff_x == offset % NX)) + coef * (same_y & (diff_x == -offset % NX))
        table += coef * (same_x & (diff_y == offset % NY)) + coef * (same_x & (diff_y == -offset % NY))
    return table


def split_table():
    table = jnp.asarray(plane_table())
    high = table.astype(BF)
    low = (table - high.astype(F32)).astype(BF)
    return jnp.concatenate([high, low], axis=0)


VMEM = pl.BlockSpec(memory_space=pltpu.VMEM)
HBM = pl.BlockSpec(memory_space=pltpu.HBM)


def near(value):
    return pltpu.with_memory_space_constraint(value, pltpu.VMEM)


def far_away(value):
    return pltpu.with_memory_space_constraint(value, pltpu.HBM)


def call(kernel, scalars, args, specs, out_shape, out_specs=None, grid=(1,), scratch=(), aliases=None):
    if out_specs is None:
        out_specs = [VMEM] * len(out_shape)
    args = [near(a) if spec is VMEM else far_away(a) if spec is HBM else a for a, spec in zip(args, specs)]
    out_shape = [pltpu.VMEM(o.shape, o.dtype) if spec is VMEM else o for o, spec in zip(out_shape, out_specs)]
    return pl.pallas_call(
        kernel,
        grid_spec=pltpu.PrefetchScalarGridSpec(
            num_scalar_prefetch=1, grid=grid, in_specs=specs, out_specs=out_specs, scratch_shapes=list(scratch)
        ),
        out_shape=out_shape,
        input_output_aliases=aliases or {},
        compiler_params=pltpu.CompilerParams(vmem_limit_bytes=16 << 20),
    )(scalars, *args)


def array(shape, kind):
    return jax.ShapeDtypeStruct(shape, kind)


def as_column(row):
    size = row.shape[1]
    diag = lax.broadcasted_iota(jnp.int32, (size, size), 0) == lax.broadcasted_iota(jnp.int32, (size, size), 1)
    spread = jnp.broadcast_to(row.astype(F32), (size, size))
    return jnp.sum(jnp.where(diag, spread, 0.0), axis=1, keepdims=True).astype(row.dtype)


def selection(column, start, width):
    lanes = lax.broadcasted_iota(jnp.int32, (column.shape[0], width), 1) + start
    return jnp.where(column == lanes, 1.0, 0.0).astype(BF)


def all_columns(rows_ref):
    return jnp.concatenate([as_column(rows_ref[p]) for p in range(4)], axis=0)


def index_kernel(ids_ref, count_ref, where_ref, meta_ref, start_ref):
    block, core, slab = ids_ref[0], ids_ref[1], ids_ref[3]
    my_y, my_x, my_z = slab // 16, (slab // 4) % 4, slab % 4
    start_ref[0] = 0

    def add(n, carry):
        start_ref[n + 1] = start_ref[n] + count_ref[block, n]
        return carry

    lax.fori_loop(0, 64, add, 0)
    for n in range(4):
        meta_ref[n] = ids_ref[n]
    lane = lax.broadcasted_iota(jnp.int32, (1, TILE), 1)
    for outer in range(4):
        for inner in range(4):
            y_step, x_step = jnp.where(core == 0, outer, inner), jnp.where(core == 0, inner, outer)
            first = (((my_y + y_step) % 4) * 4 + (my_x + x_step) % 4) * 4
            base = start_ref[first] // 8 * 8
            meta_ref[4 + outer * 4 + inner] = base
            row = jnp.full((1, TILE), -1, jnp.int32)
            for d in range(4):
                slab_d = first + (my_z + d) % 4
                begin = start_ref[slab_d]
                size = start_ref[slab_d + 1] - begin
                slot = lane - d * CAP
                row = jnp.where((slot >= 0) & (slot < size), begin - base + slot, row)
            where_ref[pl.ds(outer * 4 + inner, 1), :] = row


def index(ids, counts):
    smem = pl.BlockSpec(memory_space=pltpu.SMEM)
    return call(
        index_kernel, ids, (counts,), [smem], [array((16, TILE), jnp.int32), array((20,), jnp.int32)],
        [VMEM, smem], scratch=[pltpu.SMEM((72,), jnp.int32)],
    )


def pick_own_kernel(meta_ref, rows_ref, field_ref, out_ref, own_ref, inner_ref):
    core = meta_ref[1]
    hot = selection(as_column(rows_ref[0]), 0, ROWS)
    out_ref[...] = jnp.dot(hot, field_ref[...], preferred_element_type=F32).astype(BF)
    for half, ref in ((meta_ref[2], own_ref), (1 - meta_ref[2], inner_ref)):
        block = field_ref[pl.ds(pl.multiple_of(half * SHARE, SHARE), SHARE), :]
        ref[...] = jnp.where(core == 0, block[:, :HALF], block[:, HALF:])


def pick_own(meta, rows, field):
    return call(
        pick_own_kernel, meta, (far_away(rows), far_away(field)),
        [pl.BlockSpec((1, 1, CAP), lambda i, m: (m[0], 0, 0)), pl.BlockSpec((ROWS, NB), lambda i, m: (0, 0))],
        [array((CAP, NB), BF), array((SHARE, HALF), BF), array((SHARE, HALF), BF)],
    )


def pick_all_kernel(meta_ref, rows_ref, field_ref, fit_ref, orb_out, fit_out, hot_ref):
    @pl.when(pl.program_id(0) == 0)
    def _():
        hot_ref[...] = selection(all_columns(rows_ref), 0, ROWS)
        orb_out[...] = jnp.dot(hot_ref[...], field_ref[...], preferred_element_type=F32).astype(BF)

    at = pl.ds(pl.multiple_of(pl.program_id(0) * 512, 512), 512)
    fit_out[:, at] = jnp.dot(hot_ref[...], fit_ref[:, at], preferred_element_type=F32).astype(BF)


def pick_all(meta, rows, field, fit):
    return call(
        pick_all_kernel, meta, (rows, field, fit), [VMEM] * 3,
        [array((ALL, NB), BF), array((ALL, PTS), BF)], grid=(4,), scratch=[pltpu.VMEM((ALL, ROWS), BF)],
    )


def stencil_kernel(meta_ref, rows_ref, own_ref, inner_ref, outer_ref, pot_ref, table_ref, local_ref, *picked):
    first = meta_ref[2] == 0
    pot = pot_ref[pl.ds(pl.multiple_of(meta_ref[2] * 8, 8), 8), :]
    planes = []
    for k in range(4):
        part = pl.ds(k * PLANE, PLANE)
        planes.append(jnp.where(first, outer_ref[part, :], inner_ref[part, :]).astype(F32))
    planes += [own_ref[pl.ds(k * PLANE, PLANE), :].astype(F32) for k in range(4)]
    for k in range(4):
        part = pl.ds(k * PLANE, PLANE)
        planes.append(jnp.where(first, inner_ref[part, :], outer_ref[part, :]).astype(F32))
    for k in range(4):
        part = pl.ds(k * PLANE, PLANE)
        own = own_ref[part, :]
        center = planes[4 + k]
        total = jnp.dot(table_ref[pl.ds(0, PLANE), :], own, preferred_element_type=F32)
        total += jnp.dot(table_ref[pl.ds(PLANE, PLANE), :], own, preferred_element_type=F32)
        total += 3.0 * stencil_coef[0] * center
        for offset in range(1, 5):
            total += stencil_coef[offset] * (planes[4 + k + offset] + planes[4 + k - offset])
        scale = jnp.concatenate([as_column(pot[2 * k + n : 2 * k + n + 1, :]) for n in (0, 1)], axis=0)
        local_ref[part, :] = -0.5 * total + scale * center
    if picked:
        hot = selection(all_columns(rows_ref), meta_ref[2] * SHARE, SHARE)
        picked[0][...] = jnp.dot(hot, local_ref[...].astype(BF), preferred_element_type=F32)


def stencil(meta, rows, own, inner, outer, potential, table, with_pick):
    shapes = [array((SHARE, HALF), F32)]
    if with_pick:
        shapes.append(array((ALL, HALF), F32))
    return call(stencil_kernel, meta, (rows, own, inner, outer, potential, table), [VMEM] * 6, shapes)


def place(meta_ref, where_ref, sum_ref, group, rows):
    line = lax.broadcasted_iota(jnp.int32, (WIN, TILE), 0)
    hot = jnp.where(where_ref[pl.ds(group, 1), :] == line, 1.0, 0.0).astype(BF)
    at = pl.multiple_of(meta_ref[4 + group], 8)
    sum_ref[pl.ds(at, WIN), :] += jnp.dot(hot, rows, preferred_element_type=F32)


def place_early_kernel(meta_ref, where_ref, line_ref, up_ref, down_ref, sum_ref):
    sum_ref[...] = jnp.zeros_like(sum_ref)
    for part, ref in ((0, line_ref), (1, up_ref), (3, down_ref)):
        def step(e, carry):
            rows = ref[pl.ds(pl.multiple_of(e * TILE, TILE), TILE), :]
            place(meta_ref, where_ref, sum_ref, part * 4 + e, rows)
            return carry

        lax.fori_loop(0, 4, step, 0)


def place_early(meta, where, line, up, down):
    return call(place_early_kernel, meta, (where, line, up, down), [VMEM] * 4, [array((PTS + WIN, NB), F32)])[0]


def place_late(meta_ref, where_ref, left_ref, right_ref, sum_ref, psi_ref):
    for e in range(4):
        ref = left_ref if e < 2 else right_ref
        place(meta_ref, where_ref, sum_ref, 8 + e, ref[pl.ds((e % 2) * TILE, TILE), :])
    psi_ref[...] = sum_ref[pl.ds(0, PTS), :].astype(BF)


def place_late_kernel(meta_ref, where_ref, left_ref, right_ref, early_ref, sum_ref, psi_ref):
    place_late(meta_ref, where_ref, left_ref, right_ref, sum_ref, psi_ref)


def listed_kernel(meta_ref, where_ref, left_ref, right_ref, early_ref, orb_ref, fit_ref, local_ref,
                  sum_ref, psi_ref, keep_ref, gone_ref):
    place_late(meta_ref, where_ref, left_ref, right_ref, sum_ref, psi_ref)
    density = lax.dot_general(orb_ref[...], psi_ref[...], (((1,), (1,)), ((), ())), preferred_element_type=F32)
    kern = (fit_ref[...].astype(F32) * density).astype(BF)
    part = -jnp.dot(kern, psi_ref[...], preferred_element_type=F32)
    core = meta_ref[1]
    first = meta_ref[2] == 0
    local = local_ref[...]
    part = jnp.concatenate(
        [part[:, :HALF] + jnp.where(core == 0, local, 0.0), part[:, HALF:] + jnp.where(core == 0, 0.0, local)], axis=1
    )
    mine = [jnp.where(core == 0, part[c * 128 : c * 128 + CAP], part[c * 128 + CAP : c * 128 + 128]) for c in (0, 1)]
    other = [jnp.where(core == 0, part[c * 128 + CAP : c * 128 + 128], part[c * 128 : c * 128 + CAP]) for c in (0, 1)]
    keep_ref[:CAP, :] = jnp.where(first, mine[0], mine[1])
    keep_ref[CAP:, :] = jnp.where(first, mine[1], mine[0])
    gone_ref[:CAP, :] = jnp.where(first, other[0], other[1]).astype(BF)
    gone_ref[CAP:, :] = jnp.where(first, other[1], other[0]).astype(BF)


def listed(meta, where, left, right, early, orb, fit, local):
    return call(
        listed_kernel, meta, (where, left, right, early, orb, fit, local), [VMEM] * 7,
        [array((PTS + WIN, NB), F32), array((PTS, NB), BF), array((2 * CAP, NB), F32), array((2 * CAP, NB), BF)],
        aliases={4: 0},
    )[1:]


def pair_kernel(meta_ref, keep_ref, got_ref, near_ref, far_ref):
    near_ref[...] = keep_ref[:CAP, :] + got_ref[:CAP, :].astype(F32)
    far_ref[...] = (keep_ref[CAP:, :] + got_ref[CAP:, :].astype(F32)).astype(BF)


def pair_up(meta, keep, got):
    return call(pair_kernel, meta, (keep, got), [VMEM] * 2, [array((CAP, NB), F32), array((CAP, NB), BF)])


def update_kernel(meta_ref, near_ref, far_ref, old_ref, new_ref):
    applied = near_ref[...] + far_ref[...].astype(F32)
    new_ref[...] = ((applied - 3.5 * old_ref[...].astype(F32)) / 4.0).astype(BF)


def update_points(meta, near_part, far_part, old):
    return call(update_kernel, meta, (near_part, far_part, old), [VMEM] * 3, [array((CAP, NB), BF)])[0]


def stage_kernel(meta_ref, fit_ref, out_ref, sem):
    copy = pltpu.make_async_copy(fit_ref, out_ref, sem)
    copy.start()
    copy.wait()


def stage(meta, fit):
    return call(
        stage_kernel, meta, (fit,), [HBM], [array((ROWS, PTS), BF)],
        scratch=[pltpu.SemaphoreType.DMA],
    )[0]


def join_kernel(meta_ref, *refs):
    size = refs[0].shape[0]
    for n, ref in enumerate(refs[:-1]):
        refs[-1][pl.ds(n * size, size), :] = ref[...]


def join(meta, parts):
    shape = (len(parts) * parts[0].shape[0], NB)
    return call(join_kernel, meta, parts, [VMEM] * len(parts), [array(shape, BF)])[0]


def halves_kernel(meta_ref, up_ref, down_ref, left_ref, right_ref):
    left_ref[...] = up_ref[: 2 * TILE, :]
    right_ref[...] = down_ref[2 * TILE :, :]


def halves(meta, up, down):
    return call(halves_kernel, meta, (up, down), [VMEM] * 2, [array((2 * TILE, NB), BF)] * 2)


def finish_points(meta, where, left, right, early):
    return call(
        place_late_kernel, meta, (where, left, right, early), [VMEM] * 4,
        [array((PTS + WIN, NB), F32), array((PTS, NB), BF)], aliases={4: 0},
    )[1]


def emit(meta_ref, part, keep_ref, send_ref, at):
    core = meta_ref[1]
    left, right = part[:, :HALF], part[:, HALF:]
    keep_ref[at, :] = jnp.where(core == 0, left, right)
    send_ref[at, :] = jnp.where(core == 0, right, left).astype(BF)


def build_with(away):
    def build_kernel(meta_ref, psi_ref, orb_ref, fit_ref, kern_ref, keep_ref, send_ref):
        step = pl.program_id(0)
        half = 1 - meta_ref[2] if away else meta_ref[2]
        at = pl.ds(pl.multiple_of(step * TILE, TILE), TILE)
        rows = pl.ds(pl.multiple_of(half * SHARE + step * TILE, TILE), TILE)
        density = lax.dot_general(
            orb_ref[rows, :], psi_ref[...], (((1,), (1,)), ((), ())), preferred_element_type=F32
        )
        kern = (fit_ref[rows, :].astype(F32) * density).astype(BF)
        kern_ref[at, :] = kern
        emit(meta_ref, -jnp.dot(kern, psi_ref[...], preferred_element_type=F32), keep_ref, send_ref, at)

    return build_kernel


def build(meta, psi, orb, fit, away):
    return call(
        build_with(away), meta, (psi, orb, fit), [VMEM] * 3,
        [array((SHARE, PTS), BF), array((SHARE, HALF), F32), array((SHARE, HALF), BF)], grid=(4,),
    )


def apply_with(first, count):
    def apply_kernel(meta_ref, psi_ref, kern_ref, keep_ref, send_ref):
        def rows(step, carry):
            at = pl.ds(pl.multiple_of((first + step) * TILE, TILE), TILE)
            part = -jnp.dot(kern_ref[at, :], psi_ref[...], preferred_element_type=F32)
            emit(meta_ref, part, keep_ref, send_ref, pl.ds(pl.multiple_of(step * TILE, TILE), TILE))
            return carry

        lax.fori_loop(0, count, rows, 0)

    return apply_kernel


def apply(meta, psi, kern, first, count):
    rows = count * TILE
    return call(
        apply_with(first, count), meta, (psi, kern), [VMEM, VMEM],
        [array((rows, HALF), F32), array((rows, HALF), BF)],
    )


def sum_kernel(meta_ref, keep_ref, got_ref, sum_ref):
    sum_ref[...] = (keep_ref[...] + got_ref[...].astype(F32)).astype(BF)


def sum_away(meta, keep, got):
    return call(sum_kernel, meta, (keep, got), [VMEM] * 2, [array(keep.shape, BF)])[0]


def field_with(rows):
    def field_kernel(meta_ref, local_ref, keep_ref, core_ref, chip_ref, field_ref, *rest):
        current = field_ref[rows, :].astype(F32)
        reduced = keep_ref[rows, :] + core_ref[rows, :].astype(F32) + chip_ref[...].astype(F32)
        scaled = local_ref[rows, :] + reduced - 3.5 * current
        if len(rest) == 1:
            rest[0][...] = (scaled / 4.0).astype(BF)
        else:
            rest[1][...] = (0.5 * scaled - rest[0][rows, :].astype(F32)).astype(BF)

    return field_kernel


def next_field(meta, local, parts, fields, first):
    size = parts[2].shape[0]
    return call(
        field_with(pl.ds(first, size)), meta, (local, *parts, *fields), [VMEM] * (4 + len(fields)),
        [array((size, HALF), BF)],
    )[0]


def assemble_kernel(meta_ref, *refs):
    out_ref = refs[8]
    row = pl.program_id(0)
    first = meta_ref[1] == 0
    mine = (row // 2) == meta_ref[2]
    for part in (0, 1):
        for chunk in (0, 1):
            @pl.when((mine if part == 0 else jnp.logical_not(mine)) & (row % 2 == chunk))
            def _():
                own = refs[part * 4 + chunk][...]
                theirs = refs[part * 4 + 2 + chunk][...]
                out_ref[:, :HALF] = jnp.where(first, own, theirs)
                out_ref[:, HALF:] = jnp.where(first, theirs, own)


def assemble(meta, parts):
    return call(
        assemble_kernel, meta, parts, [VMEM] * 8, [array((ROWS, NB), BF)],
        [pl.BlockSpec((512, NB), lambda i, m: (i, 0))], grid=(4,),
    )[0]


def after(value, *earlier):
    return lax.optimization_barrier((value,) + earlier)[0]


def gather_column(meta, own):
    parts = [own] + [lax.ppermute(own, "slab", z_shift(d)) for d in (1, 2, 3)]
    return join(meta, parts)


def gather_line(meta, column):
    parts = [column] + [lax.ppermute(column, BOTH, plane_shift(d, False)) for d in (1, 2, 3)]
    return join(meta, parts)


def gather_sides(line):
    return (lax.ppermute(line, BOTH, plane_shift(1, True)), lax.ppermute(line, BOTH, plane_shift(-1, True)))


def gather_far(meta, up, down):
    near_up, near_down = halves(meta, up, down)
    left = lax.ppermute(near_up, BOTH, plane_shift(1, True))
    right = lax.ppermute(near_down, BOTH, plane_shift(-1, True))
    return left, right


def body(orbitals, potential, fit_matrix, owner_rows, owner_count):
    point_block = lax.axis_index("pt")
    slab = lax.axis_index("slab")
    core = point_block % 2
    chip = point_block // 2
    ids = jnp.stack([point_block, core, chip, slab]).astype(jnp.int32)
    table = split_table()

    own0, field0, inner0 = pick_own(ids, owner_rows, orbitals)
    potential_rows = potential.reshape(16, 128)
    column0 = gather_column(ids, own0)
    fit = stage(ids, after(fit_matrix, column0, inner0))
    line0 = gather_line(ids, column0)
    up0, down0 = gather_sides(line0)
    where, meta = index(ids, after(owner_count, up0))
    left0, right0 = gather_far(ids, up0, down0)

    outer0 = lax.ppermute(field0, BOTH, EDGE_SWAP)
    orb_listed, fit_listed = pick_all(ids, after(owner_rows, line0), orbitals, fit)
    local0, local_listed = stencil(ids, owner_rows, field0, inner0, outer0, potential_rows, table, True)

    early0 = place_early(meta, where, line0, up0, down0)
    psi0, keep, gone = listed(meta, where, left0, right0, early0, orb_listed, fit_listed, local_listed)

    near_part, far_part = pair_up(ids, keep, lax.ppermute(gone, "pt", CORE_SWAP))
    other_part = lax.ppermute(far_part, "pt", CHIP_SWAP)
    own1 = update_points(ids, near_part, other_part, own0)
    column1 = gather_column(ids, own1)
    line1 = gather_line(ids, column1)
    up1, down1 = gather_sides(line1)
    left1, right1 = gather_far(ids, up1, down1)

    def send_away(keep, gone):
        total = sum_away(ids, keep, lax.ppermute(gone, "pt", CORE_SWAP))
        return lax.ppermute(total, "pt", CHIP_SWAP)

    def own_parts(keep, gone, away):
        return keep, lax.ppermute(gone, "pt", CORE_SWAP), away

    kern_away, keep, gone = build(meta, after(psi0, far_part), orbitals, fit, True)
    away = send_away(keep, gone)
    kern_own, keep, gone = build(meta, after(psi0, line1), orbitals, fit, False)
    field1 = next_field(ids, local0, own_parts(keep, gone, away), (field0,), 0)
    inner1 = lax.ppermute(field1, "pt", CHIP_SWAP)
    outer1 = lax.ppermute(field1, BOTH, EDGE_SWAP)
    local1 = stencil(ids, owner_rows, field1, inner1, outer1, potential_rows, table, False)[0]

    early1 = place_early(meta, where, line1, up1, down1)
    psi1 = finish_points(meta, where, left1, right1, early1)
    keep_a, gone_a = apply(meta, psi1, kern_away, 0, 2)
    keep_b, gone_b = apply(meta, after(psi1, keep_a), kern_away, 2, 2)
    away_a = send_away(keep_a, gone_a)
    away_b = send_away(keep_b, gone_b)
    keep, gone = apply(meta, after(psi1, keep_b), kern_own, 0, 4)
    got = lax.ppermute(gone, "pt", CORE_SWAP)
    mine, theirs = [], []
    for n, away in enumerate((away_a, away_b)):
        field2 = next_field(ids, local1, (keep, got, away), (field1, field0), 512 * n)
        other = lax.ppermute(field2, "pt", CHIP_SWAP)
        mine += [field2, lax.ppermute(field2, "pt", CORE_SWAP)]
        theirs += [other, lax.ppermute(other, "pt", CORE_SWAP)]
    parts = [mine[0], mine[2], mine[1], mine[3], theirs[0], theirs[2], theirs[1], theirs[3]]
    return assemble(ids, parts)


def solution(mesh):
    placed = (P("slab", None), P("slab"), P("slab", "pt"), P(None, "slab", None), P())
    return jax.shard_map(body, mesh=mesh, in_specs=placed, out_specs=P("slab", None), check_vma=False)
```

```python
import jax
import jax.numpy as jnp
import numpy as np
from jax import lax
from jax.experimental import pallas as pl
from jax.experimental.pallas import tpu as pltpu
from jax.sharding import PartitionSpec as P


NB = 256
HALF = 128
NY = 8
NX = 32
PLANE = NY * NX
ROWS = 2048
SHARE = 1024
PTS = 2048
CAP = 64
ALL = 4 * CAP
WIN = 272
TILE = 256
BF = jnp.bfloat16
F32 = jnp.float32

stencil_coef = (-205.0 / 72.0, 8.0 / 5.0, -1.0 / 5.0, 8.0 / 315.0, -1.0 / 560.0)


def slab_id(y, x, z):
    return ((y % 4) * 4 + (x % 4)) * 4 + (z % 4)


def z_shift(d):
    return [(slab_id(y, x, z), slab_id(y, x, z - d)) for y in range(4) for x in range(4) for z in range(4)]


def plane_shift(d, second):
    pairs = []
    for y in range(4):
        for x in range(4):
            for z in range(4):
                for p in range(4):
                    along_x = (p % 2 == 0) != second
                    target = slab_id(y, x - d, z) if along_x else slab_id(y - d, x, z)
                    pairs.append((slab_id(y, x, z) * 4 + p, target * 4 + p))
    return pairs


BOTH = ("slab", "pt")
CORE_SWAP = [(i, i ^ 1) for i in range(4)]
CHIP_SWAP = [(i, i ^ 2) for i in range(4)]
EDGE_SWAP = [(s * 4 + 2 + c, ((s + 1) % 64) * 4 + c) for s in range(64) for c in range(2)] + [
    (s * 4 + c, ((s - 1) % 64) * 4 + 2 + c) for s in range(64) for c in range(2)
]


def plane_table():
    cell_ids = np.arange(PLANE)
    row_y = cell_ids // NX
    col_x = cell_ids % NX
    diff_y = (row_y[:, None] - row_y[None, :]) % NY
    diff_x = (col_x[:, None] - col_x[None, :]) % NX
    same_y = row_y[:, None] == row_y[None, :]
    same_x = col_x[:, None] == col_x[None, :]
    table = np.zeros((PLANE, PLANE), np.float32)
    for offset in range(1, 5):
        coef = np.float32(stencil_coef[offset])
        table += coef * (same_y & (diff_x == offset % NX)) + coef * (same_y & (diff_x == -offset % NX))
        table += coef * (same_x & (diff_y == offset % NY)) + coef * (same_x & (diff_y == -offset % NY))
    return table


def split_table():
    table = jnp.asarray(plane_table())
    high = table.astype(BF)
    low = (table - high.astype(F32)).astype(BF)
    return jnp.concatenate([high, low], axis=0)


VMEM = pl.BlockSpec(memory_space=pltpu.VMEM)
HBM = pl.BlockSpec(memory_space=pltpu.HBM)


def near(value):
    return pltpu.with_memory_space_constraint(value, pltpu.VMEM)


def far_away(value):
    return pltpu.with_memory_space_constraint(value, pltpu.HBM)


def call(kernel, scalars, args, specs, out_shape, out_specs=None, grid=(1,), scratch=(), aliases=None):
    if out_specs is None:
        out_specs = [VMEM] * len(out_shape)
    args = [near(a) if spec is VMEM else far_away(a) if spec is HBM else a for a, spec in zip(args, specs)]
    out_shape = [pltpu.VMEM(o.shape, o.dtype) if spec is VMEM else o for o, spec in zip(out_shape, out_specs)]
    return pl.pallas_call(
        kernel,
        grid_spec=pltpu.PrefetchScalarGridSpec(
            num_scalar_prefetch=1, grid=grid, in_specs=specs, out_specs=out_specs, scratch_shapes=list(scratch)
        ),
        out_shape=out_shape,
        input_output_aliases=aliases or {},
        compiler_params=pltpu.CompilerParams(vmem_limit_bytes=16 << 20),
    )(scalars, *args)


def array(shape, kind):
    return jax.ShapeDtypeStruct(shape, kind)


def as_column(row):
    size = row.shape[1]
    diag = lax.broadcasted_iota(jnp.int32, (size, size), 0) == lax.broadcasted_iota(jnp.int32, (size, size), 1)
    spread = jnp.broadcast_to(row.astype(F32), (size, size))
    return jnp.sum(jnp.where(diag, spread, 0.0), axis=1, keepdims=True).astype(row.dtype)


def selection(column, start, width):
    lanes = lax.broadcasted_iota(jnp.int32, (column.shape[0], width), 1) + start
    return jnp.where(column == lanes, 1.0, 0.0).astype(BF)


def all_columns(rows_ref):
    return jnp.concatenate([as_column(rows_ref[p]) for p in range(4)], axis=0)


def index_kernel(ids_ref, count_ref, where_ref, meta_ref, start_ref):
    block, core, slab = ids_ref[0], ids_ref[1], ids_ref[3]
    my_y, my_x, my_z = slab // 16, (slab // 4) % 4, slab % 4
    start_ref[0] = 0

    def add(n, carry):
        start_ref[n + 1] = start_ref[n] + count_ref[block, n]
        return carry

    lax.fori_loop(0, 64, add, 0)
    for n in range(4):
        meta_ref[n] = ids_ref[n]
    lane = lax.broadcasted_iota(jnp.int32, (1, TILE), 1)
    for outer in range(4):
        for inner in range(4):
            y_step, x_step = jnp.where(core == 0, outer, inner), jnp.where(core == 0, inner, outer)
            first = (((my_y + y_step) % 4) * 4 + (my_x + x_step) % 4) * 4
            base = start_ref[first] // 8 * 8
            meta_ref[4 + outer * 4 + inner] = base
            row = jnp.full((1, TILE), -1, jnp.int32)
            for d in range(4):
                slab_d = first + (my_z + d) % 4
                begin = start_ref[slab_d]
                size = start_ref[slab_d + 1] - begin
                slot = lane - d * CAP
                row = jnp.where((slot >= 0) & (slot < size), begin - base + slot, row)
            where_ref[pl.ds(outer * 4 + inner, 1), :] = row


def index(ids, counts):
    smem = pl.BlockSpec(memory_space=pltpu.SMEM)
    return call(
        index_kernel, ids, (counts,), [smem], [array((16, TILE), jnp.int32), array((20,), jnp.int32)],
        [VMEM, smem], scratch=[pltpu.SMEM((72,), jnp.int32)],
    )


def pick_own_kernel(meta_ref, rows_ref, field_ref, out_ref, own_ref, inner_ref):
    core = meta_ref[1]
    hot = selection(as_column(rows_ref[0]), 0, ROWS)
    out_ref[...] = jnp.dot(hot, field_ref[...], preferred_element_type=F32).astype(BF)
    for half, ref in ((meta_ref[2], own_ref), (1 - meta_ref[2], inner_ref)):
        block = field_ref[pl.ds(pl.multiple_of(half * SHARE, SHARE), SHARE), :]
        ref[...] = jnp.where(core == 0, block[:, :HALF], block[:, HALF:])


def pick_own(meta, rows, field):
    return call(
        pick_own_kernel, meta, (far_away(rows), far_away(field)),
        [pl.BlockSpec((1, 1, CAP), lambda i, m: (m[0], 0, 0)), pl.BlockSpec((ROWS, NB), lambda i, m: (0, 0))],
        [array((CAP, NB), BF), array((SHARE, HALF), BF), array((SHARE, HALF), BF)],
    )


def pick_all_kernel(meta_ref, rows_ref, field_ref, fit_ref, orb_out, fit_out, hot_ref):
    @pl.when(pl.program_id(0) == 0)
    def _():
        hot_ref[...] = selection(all_columns(rows_ref), 0, ROWS)
        orb_out[...] = jnp.dot(hot_ref[...], field_ref[...], preferred_element_type=F32).astype(BF)

    at = pl.ds(pl.multiple_of(pl.program_id(0) * 512, 512), 512)
    fit_out[:, at] = jnp.dot(hot_ref[...], fit_ref[:, at], preferred_element_type=F32).astype(BF)


def pick_all(meta, rows, field, fit):
    return call(
        pick_all_kernel, meta, (rows, field, fit), [VMEM] * 3,
        [array((ALL, NB), BF), array((ALL, PTS), BF)], grid=(4,), scratch=[pltpu.VMEM((ALL, ROWS), BF)],
    )


def stencil_kernel(meta_ref, rows_ref, own_ref, inner_ref, outer_ref, pot_ref, table_ref, local_ref, *picked):
    first = meta_ref[2] == 0
    pot = pot_ref[pl.ds(pl.multiple_of(meta_ref[2] * 8, 8), 8), :]
    planes = []
    for k in range(4):
        part = pl.ds(k * PLANE, PLANE)
        planes.append(jnp.where(first, outer_ref[part, :], inner_ref[part, :]).astype(F32))
    planes += [own_ref[pl.ds(k * PLANE, PLANE), :].astype(F32) for k in range(4)]
    for k in range(4):
        part = pl.ds(k * PLANE, PLANE)
        planes.append(jnp.where(first, inner_ref[part, :], outer_ref[part, :]).astype(F32))
    for k in range(4):
        part = pl.ds(k * PLANE, PLANE)
        own = own_ref[part, :]
        center = planes[4 + k]
        total = jnp.dot(table_ref[pl.ds(0, PLANE), :], own, preferred_element_type=F32)
        total += jnp.dot(table_ref[pl.ds(PLANE, PLANE), :], own, preferred_element_type=F32)
        total += 3.0 * stencil_coef[0] * center
        for offset in range(1, 5):
            total += stencil_coef[offset] * (planes[4 + k + offset] + planes[4 + k - offset])
        scale = jnp.concatenate([as_column(pot[2 * k + n : 2 * k + n + 1, :]) for n in (0, 1)], axis=0)
        local_ref[part, :] = -0.5 * total + scale * center
    if picked:
        hot = selection(all_columns(rows_ref), meta_ref[2] * SHARE, SHARE)
        picked[0][...] = jnp.dot(hot, local_ref[...].astype(BF), preferred_element_type=F32)


def stencil(meta, rows, own, inner, outer, potential, table, with_pick):
    shapes = [array((SHARE, HALF), F32)]
    if with_pick:
        shapes.append(array((ALL, HALF), F32))
    return call(stencil_kernel, meta, (rows, own, inner, outer, potential, table), [VMEM] * 6, shapes)


def place(meta_ref, where_ref, sum_ref, group, rows):
    line = lax.broadcasted_iota(jnp.int32, (WIN, TILE), 0)
    hot = jnp.where(where_ref[pl.ds(group, 1), :] == line, 1.0, 0.0).astype(BF)
    at = pl.multiple_of(meta_ref[4 + group], 8)
    sum_ref[pl.ds(at, WIN), :] += jnp.dot(hot, rows, preferred_element_type=F32)


def place_early_kernel(meta_ref, where_ref, line_ref, up_ref, down_ref, sum_ref):
    sum_ref[...] = jnp.zeros_like(sum_ref)
    for part, ref in ((0, line_ref), (1, up_ref), (3, down_ref)):
        def step(e, carry):
            rows = ref[pl.ds(pl.multiple_of(e * TILE, TILE), TILE), :]
            place(meta_ref, where_ref, sum_ref, part * 4 + e, rows)
            return carry

        lax.fori_loop(0, 4, step, 0)


def place_early(meta, where, line, up, down):
    return call(
        place_early_kernel, meta, (where, line, up, down),
        [VMEM] * 4, [array((PTS + WIN, NB), F32)],
    )[0]


def place_late(meta_ref, where_ref, left_ref, right_ref, sum_ref, psi_ref):
    for e in range(4):
        ref = left_ref if e < 2 else right_ref
        place(meta_ref, where_ref, sum_ref, 8 + e, ref[pl.ds((e % 2) * TILE, TILE), :])
    psi_ref[...] = sum_ref[pl.ds(0, PTS), :].astype(BF)


def place_late_kernel(meta_ref, where_ref, left_ref, right_ref, early_ref, sum_ref, psi_ref):
    place_late(meta_ref, where_ref, left_ref, right_ref, sum_ref, psi_ref)


def listed_kernel(meta_ref, where_ref, left_ref, right_ref, early_ref, orb_ref, fit_ref, local_ref,
                  sum_ref, psi_ref, keep_ref, gone_ref):
    place_late(meta_ref, where_ref, left_ref, right_ref, sum_ref, psi_ref)
    density = lax.dot_general(orb_ref[...], psi_ref[...], (((1,), (1,)), ((), ())), preferred_element_type=F32)
    kern = (fit_ref[...].astype(F32) * density).astype(BF)
    part = -jnp.dot(kern, psi_ref[...], preferred_element_type=F32)
    core = meta_ref[1]
    first = meta_ref[2] == 0
    local = local_ref[...]
    part = jnp.concatenate(
        [part[:, :HALF] + jnp.where(core == 0, local, 0.0), part[:, HALF:] + jnp.where(core == 0, 0.0, local)], axis=1
    )
    mine = [jnp.where(core == 0, part[c * 128 : c * 128 + CAP], part[c * 128 + CAP : c * 128 + 128]) for c in (0, 1)]
    other = [jnp.where(core == 0, part[c * 128 + CAP : c * 128 + 128], part[c * 128 : c * 128 + CAP]) for c in (0, 1)]
    keep_ref[:CAP, :] = jnp.where(first, mine[0], mine[1])
    keep_ref[CAP:, :] = jnp.where(first, mine[1], mine[0])
    gone_ref[:CAP, :] = jnp.where(first, other[0], other[1]).astype(BF)
    gone_ref[CAP:, :] = jnp.where(first, other[1], other[0]).astype(BF)


def listed(meta, where, left, right, early, orb, fit, local):
    return call(
        listed_kernel, meta, (where, left, right, early, orb, fit, local), [VMEM] * 7,
        [array((PTS + WIN, NB), F32), array((PTS, NB), BF), array((2 * CAP, NB), F32), array((2 * CAP, NB), BF)],
        aliases={4: 0},
    )[1:]


def pair_kernel(meta_ref, keep_ref, got_ref, near_ref, far_ref):
    near_ref[...] = keep_ref[:CAP, :] + got_ref[:CAP, :].astype(F32)
    far_ref[...] = (keep_ref[CAP:, :] + got_ref[CAP:, :].astype(F32)).astype(BF)


def pair_up(meta, keep, got):
    return call(pair_kernel, meta, (keep, got), [VMEM] * 2, [array((CAP, NB), F32), array((CAP, NB), BF)])


def update_kernel(meta_ref, near_ref, far_ref, old_ref, new_ref):
    applied = near_ref[...] + far_ref[...].astype(F32)
    new_ref[...] = ((applied - 3.5 * old_ref[...].astype(F32)) / 4.0).astype(BF)


def update_points(meta, near_part, far_part, old):
    return call(update_kernel, meta, (near_part, far_part, old), [VMEM] * 3, [array((CAP, NB), BF)])[0]


def stage_kernel(meta_ref, fit_ref, out_ref, sem):
    copy = pltpu.make_async_copy(fit_ref, out_ref, sem)
    copy.start()
    copy.wait()


def stage(meta, fit):
    return call(
        stage_kernel, meta, (fit,), [HBM], [array((ROWS, PTS), BF)],
        scratch=[pltpu.SemaphoreType.DMA],
    )[0]


def join_kernel(meta_ref, *refs):
    size = refs[0].shape[0]
    for n, ref in enumerate(refs[:-1]):
        refs[-1][pl.ds(n * size, size), :] = ref[...]


def join(meta, parts):
    shape = (len(parts) * parts[0].shape[0], NB)
    return call(join_kernel, meta, parts, [VMEM] * len(parts), [array(shape, BF)])[0]


def halves_kernel(meta_ref, up_ref, down_ref, left_ref, right_ref):
    left_ref[...] = up_ref[: 2 * TILE, :]
    right_ref[...] = down_ref[2 * TILE :, :]


def halves(meta, up, down):
    return call(halves_kernel, meta, (up, down), [VMEM] * 2, [array((2 * TILE, NB), BF)] * 2)


def finish_points(meta, where, left, right, early):
    return call(
        place_late_kernel, meta, (where, left, right, early), [VMEM] * 4,
        [array((PTS + WIN, NB), F32), array((PTS, NB), BF)], aliases={4: 0},
    )[1]


def emit(meta_ref, part, keep_ref, send_ref, at):
    core = meta_ref[1]
    left, right = part[:, :HALF], part[:, HALF:]
    keep_ref[at, :] = jnp.where(core == 0, left, right)
    send_ref[at, :] = jnp.where(core == 0, right, left).astype(BF)


def build_with(away):
    def build_kernel(meta_ref, psi_ref, orb_ref, fit_ref, kern_ref, keep_ref, send_ref):
        step = pl.program_id(0)
        half = 1 - meta_ref[2] if away else meta_ref[2]
        at = pl.ds(pl.multiple_of(step * TILE, TILE), TILE)
        rows = pl.ds(pl.multiple_of(half * SHARE + step * TILE, TILE), TILE)
        density = lax.dot_general(
            orb_ref[rows, :], psi_ref[...], (((1,), (1,)), ((), ())), preferred_element_type=F32
        )
        kern = (fit_ref[rows, :].astype(F32) * density).astype(BF)
        kern_ref[at, :] = kern
        emit(meta_ref, -jnp.dot(kern, psi_ref[...], preferred_element_type=F32), keep_ref, send_ref, at)

    return build_kernel


def build(meta, psi, orb, fit, away):
    return call(
        build_with(away), meta, (psi, orb, fit), [VMEM] * 3,
        [array((SHARE, PTS), BF), array((SHARE, HALF), F32), array((SHARE, HALF), BF)], grid=(4,),
    )


def tile_start(step):
    return step * TILE if isinstance(step, int) else pl.multiple_of(step * TILE, TILE)


def apply_with(first, count):
    def apply_kernel(meta_ref, psi_ref, kern_ref, keep_ref, send_ref):
        def rows(step, carry):
            at = pl.ds(tile_start(first + step), TILE)
            part = -jnp.dot(kern_ref[at, :], psi_ref[...], preferred_element_type=F32)
            emit(meta_ref, part, keep_ref, send_ref, pl.ds(tile_start(step), TILE))
            return carry

        if count == 2:
            rows(1, rows(0, 0))
        else:
            lax.fori_loop(0, count, rows, 0)

    return apply_kernel


def apply(meta, psi, kern, first, count):
    rows = count * TILE
    return call(
        apply_with(first, count), meta, (psi, kern), [VMEM, VMEM],
        [array((rows, HALF), F32), array((rows, HALF), BF)],
    )


def sum_kernel(meta_ref, keep_ref, got_ref, sum_ref):
    sum_ref[...] = (keep_ref[...] + got_ref[...].astype(F32)).astype(BF)


def sum_away(meta, keep, got):
    return call(sum_kernel, meta, (keep, got), [VMEM] * 2, [array(keep.shape, BF)])[0]


def join_field_kernel(meta_ref, local_ref, keep_ref, core_ref, chip_ref, field_ref, old_ref, done_ref, new_ref, whole_ref):
    field_with(pl.ds(512, 512))(
        meta_ref, local_ref, keep_ref, core_ref, chip_ref, field_ref, old_ref, new_ref
    )
    whole_ref[:512, :] = done_ref[...]
    whole_ref[512:, :] = new_ref[...]


def join_field(meta, local, parts, fields):
    return call(
        join_field_kernel, meta, (local, *parts, *fields), [VMEM] * 7,
        [array((512, HALF), BF), array((SHARE, HALF), BF)],
    )


def field_with(rows):
    def field_kernel(meta_ref, local_ref, keep_ref, core_ref, chip_ref, field_ref, *rest):
        current = field_ref[rows, :].astype(F32)
        reduced = keep_ref[rows, :] + core_ref[rows, :].astype(F32) + chip_ref[...].astype(F32)
        scaled = local_ref[rows, :] + reduced - 3.5 * current
        if len(rest) == 1:
            rest[0][...] = (scaled / 4.0).astype(BF)
        else:
            rest[1][...] = (0.5 * scaled - rest[0][rows, :].astype(F32)).astype(BF)

    return field_kernel


def next_field(meta, local, parts, fields, first):
    size = parts[2].shape[0]
    return call(
        field_with(pl.ds(first, size)), meta, (local, *parts, *fields), [VMEM] * (4 + len(fields)),
        [array((size, HALF), BF)],
    )[0]


def put_own_kernel(meta_ref, own_ref, mirror_ref, out_ref):
    first = meta_ref[1] == 0
    out_ref[:, :HALF] = jnp.where(first, own_ref[...], mirror_ref[...])
    out_ref[:, HALF:] = jnp.where(first, mirror_ref[...], own_ref[...])


def put_own(meta, own, mirror):
    return call(
        put_own_kernel, meta, (own, mirror), [VMEM] * 2, [array((ROWS, NB), BF)],
        [pl.BlockSpec((SHARE, NB), lambda i, m: (m[2], 0))],
    )[0]


def put_other_kernel(meta_ref, done_ref, own_a, own_b, mirror_a, mirror_b, out_ref):
    first = meta_ref[1] == 0
    for n, own, mirror in ((0, own_a, mirror_a), (1, own_b, mirror_b)):
        at = pl.ds(n * 512, 512)
        out_ref[at, :HALF] = jnp.where(first, own[...], mirror[...])
        out_ref[at, HALF:] = jnp.where(first, mirror[...], own[...])


def put_other(meta, done, *parts):
    return call(
        put_other_kernel, meta, (done, *parts), [HBM] + [VMEM] * 4, [array((ROWS, NB), BF)],
        [pl.BlockSpec((SHARE, NB), lambda i, m: (1 - m[2], 0))], aliases={1: 0},
    )[0]


def after(value, *earlier):
    return lax.optimization_barrier((value,) + earlier)[0]


def gather_column(meta, own):
    parts = [own] + [lax.ppermute(own, "slab", z_shift(d)) for d in (1, 2, 3)]
    return join(meta, parts)


def gather_line(meta, column):
    parts = [column] + [lax.ppermute(column, BOTH, plane_shift(d, False)) for d in (1, 2, 3)]
    return join(meta, parts)


def gather_sides(line):
    return (lax.ppermute(line, BOTH, plane_shift(1, True)), lax.ppermute(line, BOTH, plane_shift(-1, True)))


def gather_far(meta, up, down):
    near_up, near_down = halves(meta, up, down)
    left = lax.ppermute(near_up, BOTH, plane_shift(1, True))
    right = lax.ppermute(near_down, BOTH, plane_shift(-1, True))
    return left, right


def body(orbitals, potential, fit_matrix, owner_rows, owner_count):
    point_block = lax.axis_index("pt")
    slab = lax.axis_index("slab")
    core = point_block % 2
    chip = point_block // 2
    ids = jnp.stack([point_block, core, chip, slab]).astype(jnp.int32)
    table = split_table()

    own0, field0, inner0 = pick_own(ids, owner_rows, orbitals)
    potential_rows = potential.reshape(16, 128)
    column0 = gather_column(ids, own0)
    fit = stage(ids, after(fit_matrix, column0, inner0))
    line0 = gather_line(ids, column0)
    where, meta = index(ids, after(owner_count, column0))
    up0, down0 = gather_sides(line0)
    left0, right0 = gather_far(ids, up0, down0)

    outer0 = lax.ppermute(field0, BOTH, EDGE_SWAP)
    orb_listed, fit_listed = pick_all(ids, after(owner_rows, line0), orbitals, fit)
    local0, local_listed = stencil(ids, owner_rows, field0, inner0, outer0, potential_rows, table, True)

    early0 = place_early(meta, where, line0, up0, down0)
    psi0, keep, gone = listed(meta, where, left0, right0, early0, orb_listed, fit_listed, local_listed)

    near_part, far_part = pair_up(ids, keep, lax.ppermute(gone, "pt", CORE_SWAP))
    other_part = lax.ppermute(far_part, "pt", CHIP_SWAP)
    own1 = update_points(ids, near_part, other_part, own0)
    column1 = gather_column(ids, own1)
    line1 = gather_line(ids, column1)
    up1, down1 = gather_sides(line1)
    left1, right1 = gather_far(ids, up1, down1)

    def send_away(keep, gone):
        total = sum_away(ids, keep, lax.ppermute(gone, "pt", CORE_SWAP))
        return lax.ppermute(total, "pt", CHIP_SWAP)

    def own_parts(keep, gone, away):
        return keep, lax.ppermute(gone, "pt", CORE_SWAP), away

    kern_away, keep, gone = build(meta, after(psi0, far_part), orbitals, fit, True)
    away = send_away(keep, gone)
    kern_own, keep, gone = build(meta, after(psi0, line1), orbitals, fit, False)
    field1 = next_field(ids, local0, own_parts(keep, gone, away), (field0,), 0)
    inner1 = lax.ppermute(field1, "pt", CHIP_SWAP)
    outer1 = lax.ppermute(field1, BOTH, EDGE_SWAP)
    local1 = stencil(ids, owner_rows, field1, inner1, outer1, potential_rows, table, False)[0]

    early1 = place_early(meta, where, line1, up1, down1)
    psi1 = finish_points(meta, where, left1, right1, early1)
    keep_a, gone_a = apply(meta, psi1, kern_away, 0, 2)
    keep_b, gone_b = apply(meta, after(psi1, keep_a), kern_away, 2, 2)
    away_a = send_away(keep_a, gone_a)
    away_b = send_away(keep_b, gone_b)
    keep, gone = apply(meta, after(psi1, keep_b), kern_own, 0, 4)
    got = lax.ppermute(gone, "pt", CORE_SWAP)
    new_a = next_field(ids, local1, (keep, got, away_a), (field1, field0), 0)
    other_a = lax.ppermute(new_a, "pt", CHIP_SWAP)
    new_b, whole = join_field(ids, local1, (keep, got, away_b), (field1, field0, new_a))
    other_b = lax.ppermute(new_b, "pt", CHIP_SWAP)
    out = put_own(ids, whole, lax.ppermute(whole, "pt", CORE_SWAP))
    mirror_a = lax.ppermute(other_a, "pt", CORE_SWAP)
    mirror_b = lax.ppermute(other_b, "pt", CORE_SWAP)
    return put_other(ids, out, other_a, other_b, mirror_a, mirror_b)


def solution(mesh):
    placed = (P("slab", None), P("slab"), P("slab", "pt"), P(None, "slab", None), P())
    return jax.shard_map(body, mesh=mesh, in_specs=placed, out_specs=P("slab", None), check_vma=False)
```
